256 devices in a mesh: sub: 64 (over z, x, core), src: 4 (over y).
Axes of the slice: x: 4, y: 4, z: 8, core: 2. Of those that a mesh axis runs over, the one named last changes fastest.
Arguments:
- leaf_maps: float32 [64, 512, 512], P('sub', None, 'src'), may hold values from -3 to 12, as said below
- impedance: float32 [64, 512], P('sub'), may hold values from 0.5 to 4
- sources: float32 [64, 512, 1024], P('sub', None, 'src'), may hold values from -12 to 12
- top_trace: float32 [8, 512, 1024], P(None, None, 'src'), may hold values from -6 to 6
- interior_op: float32 [64, 1024, 512], P('sub', 'src'), may hold values from -0.25 to 0.25
Outputs:
- interior: float32 [64, 1024, 1024], P('sub', 'src')
The draws below stay inside these ranges and needn't reach their ends.
Inputs may be any that keep to these rules, and one draw needn't show every extreme that they name: `leaf_maps`: each leaf's map is symmetric with least eigenvalue 0.5 or more.
All inputs are finite; a program needn't handle non-finite values.
Results may differ from the reference program's by a relative error of at most 0.0003.
Values sent between devices are 32-bit elements; how exact they have to be, the bound alone decides.
A program may use at most 64 MiB of HBM per device.

```python
import math
from functools import partial
import jax
import jax.numpy as jnp
from jax import lax

M = 512
NSRC = 1024
CELLS = 1024
LEVELS = 3
LEAVES = 64
TOP = 8


def draw_leaf_maps(key, part):
    key_diag, key_off = jax.random.split(jax.random.fold_in(key, 17), 2)
    diagonal = jax.random.uniform(key_diag, (LEAVES, M), jnp.float32, 3.0, 6.0)
    raw = jnp.clip(jax.random.normal(key_off, (LEAVES, M, M), jnp.float32), -6.0, 6.0)
    off_diag = (raw + jnp.swapaxes(raw, 1, 2)) * (math.sqrt(0.5) / math.sqrt(M))
    maps = off_diag + diagonal[:, :, None] * jnp.eye(M, dtype=jnp.float32)[None]
    maps = maps + 8.0 / M
    return maps


def block_levels(own_key, shape, cuts, low, largest):
    gain = 1.0
    for axis_at, parts in cuts:
        steps = jax.random.uniform(jax.random.fold_in(jax.random.fold_in(own_key, 6), axis_at), (parts,), jnp.float32, low / len(cuts), largest / len(cuts))
        gain = gain * jnp.repeat(jnp.exp(steps), shape[axis_at] // parts).reshape((-1,) + (1,) * (len(shape) - 1 - axis_at))
    return gain


def scatter_about(rng, shape, scale, reach, shards=(), kind=jnp.bfloat16):
    result = jax.random.normal(rng, shape, jnp.float32) * scale
    if len(shards) > 0:
        result = block_levels(rng, shape, shards, -0.22, 0.18) * result
    return jnp.clip(result, min=-reach, max=reach).astype(kind)


def setup_inputs(seed: int = 0) -> dict:
    arg_keys = jax.random.split(jax.random.key(seed), 6)
    return {
        "leaf_maps": draw_leaf_maps(jax.random.fold_in(arg_keys[5], 71), 0),
        "impedance": jnp.clip(jnp.exp(math.log(4.0) - 2.0794415 * jax.random.uniform(arg_keys[1], (LEAVES, M), jnp.float32) ** block_levels(arg_keys[1], (LEAVES, M), ((0, 64),), -0.2, 0.2)), 0.5, 4.0),
        "sources": scatter_about(arg_keys[2], (LEAVES, M, NSRC), 2.0, 12.0, ((0, 64), (2, 4)), jnp.float32),
        "top_trace": scatter_about(arg_keys[3], (TOP, M, NSRC), 1.0, 6.0, ((2, 4),), jnp.float32),
        "interior_op": scatter_about(arg_keys[4], (LEAVES, CELLS, M), M ** -0.5, 0.25, ((0, 64), (1, 4)), jnp.float32),
    }


def reorder_rows(matrix):
    quarter = matrix.shape[0] // 4
    blocks = matrix.reshape((2, 2, quarter) + matrix.shape[1:])
    return jnp.swapaxes(blocks, 0, 1).reshape(matrix.shape)

def reorder_cols(matrix):
    row_count, col_count = matrix.shape
    quarter = col_count // 4
    blocks = matrix.reshape((row_count, 2, 2, quarter))
    return jnp.swapaxes(blocks, 1, 2).reshape((row_count, col_count))

def chol_solve(factor, right_side):
    first_pass = lax.linalg.triangular_solve(factor, right_side, left_side=True, lower=True)
    return lax.linalg.triangular_solve(factor, first_pass, left_side=True, lower=True, transpose_a=True)

def merge_pair(own_map, own_trace, other_map, other_trace, is_beta, need_parent):
    first_map = jnp.where(is_beta, other_map, own_map)
    second_map = jnp.where(is_beta, own_map, other_map)
    first_trace = jnp.where(is_beta, other_trace, own_trace)
    second_trace = jnp.where(is_beta, own_trace, other_trace)
    midpoint = first_map.shape[0] // 2
    schur_block = first_map[midpoint:, midpoint:] + second_map[midpoint:, midpoint:]
    factor = jnp.linalg.cholesky(schur_block)
    coupling = jnp.concatenate([first_map[midpoint:, :midpoint], second_map[midpoint:, :midpoint]], axis=1)
    shared = first_trace[midpoint:] + second_trace[midpoint:]
    if not need_parent:
        return (None, None, (factor, coupling, shared))
    solved = chol_solve(factor, coupling)
    shared_sol = chol_solve(factor, shared)
    filler = jnp.zeros((midpoint, midpoint), jnp.float32)
    upper_rows = jnp.concatenate([first_map[:midpoint, :midpoint], filler], axis=1)
    lower_rows = jnp.concatenate([filler, second_map[:midpoint, :midpoint]], axis=1)
    blocks = jnp.concatenate([upper_rows, lower_rows], axis=0)
    parent = blocks - jnp.dot(coupling.T, solved, precision=lax.Precision.HIGHEST)
    outer = jnp.concatenate([first_trace[:midpoint], second_trace[:midpoint]], axis=0)
    traces = outer - jnp.dot(coupling.T, shared_sol, precision=lax.Precision.HIGHEST)
    return (reorder_cols(reorder_rows(parent)), reorder_rows(traces), (factor, coupling, shared))

def descend(node_trace, factor, coupling, shared, is_beta):
    stacked = reorder_rows(node_trace)
    midpoint = stacked.shape[0] // 2
    right_side = jnp.dot(coupling, stacked, precision=lax.Precision.HIGHEST) + shared
    interior_edge = -chol_solve(factor, right_side)
    own_edge = jnp.where(is_beta, stacked[midpoint:], stacked[:midpoint])
    return jnp.concatenate([own_edge, interior_edge], axis=0)

def reference(leaf_maps, impedance, sources, top_trace, interior_op):
    node_maps = leaf_maps + impedance[:, :, None] * jnp.eye(M, dtype=jnp.float32)[None]
    node_traces = sources
    saved_levels = []
    for height in range(LEVELS):
        merger = jax.vmap(partial(merge_pair, is_beta=False, need_parent=height < LEVELS - 1))
        node_maps, node_traces, saved_level = merger(node_maps[0::2], node_traces[0::2], node_maps[1::2], node_traces[1::2])
        saved_levels.append(saved_level)
    current = top_trace
    for height in reversed(range(LEVELS)):
        factor, coupling, shared = saved_levels[height]
        first_child = jax.vmap(partial(descend, is_beta=False))(current, factor, coupling, shared)
        second_child = jax.vmap(partial(descend, is_beta=True))(current, factor, coupling, shared)
        current = jnp.stack([first_child, second_child], axis=1).reshape((-1,) + first_child.shape[1:])
    apply_op = jax.vmap(partial(jnp.dot, precision=lax.Precision.HIGHEST))
    return apply_op(interior_op, current)
```

```python
import functools

import jax
import jax.numpy as jnp
from jax import lax
from jax.experimental import pallas as pl
from jax.experimental.pallas import tpu as pltpu
from jax.sharding import PartitionSpec as P

F32 = jnp.float32
MESH = pl.DeviceIdType.MESH
NN = ((1,), (0,))
TN = ((0,), (0,))
NT = ((1,), (1,))
NSEM = 256


def mm(a, b, dims=NN):
    return lax.dot_general(
        a, b, (dims, ((), ())), precision=lax.Precision.HIGHEST, preferred_element_type=F32
    )


def inverse_2(p):
    a, b, d = p[0][0], p[0][1], p[1][1]
    r = 1.0 / (a * d - b * b)
    off = -(b * r)
    return [[d * r, off], [off, a * r]]


def small_mm(x, y):
    return [
        [sum((x[i][k] * y[k][j] for k in range(1, len(y))), x[i][0] * y[0][j]) for j in range(len(y[0]))]
        for i in range(len(x))
    ]


def flip(x):
    return [[x[i][j] for i in range(len(x))] for j in range(len(x[0]))]


def inverse_4(p):
    a = inverse_2([r[:2] for r in p[:2]])
    b = [r[2:] for r in p[:2]]
    w = small_mm(a, b)
    bw = small_mm(flip(b), w)
    s = inverse_2([[p[2 + i][2 + j] - bw[i][j] for j in range(2)] for i in range(2)])
    ws = small_mm(w, s)
    c = small_mm(ws, flip(w))
    top = [[a[i][0] + c[i][0], a[i][1] + c[i][1], -ws[i][0], -ws[i][1]] for i in range(2)]
    low = [[-ws[0][i], -ws[1][i], s[i][0], s[i][1]] for i in range(2)]
    return top + low


def invert_tiles(m, start, stop):
    n = m.shape[0]
    lane = lax.broadcasted_iota(jnp.int32, (1, n), 1)
    sub8 = lax.broadcasted_iota(jnp.int32, (8, 1), 0)

    def body(t, carry):
        r0 = pl.multiple_of(t * 8, 8)
        for q in range(0, 8, 4):
            k = t * 8 + q
            whole = m[...]
            tile = m[pl.ds(r0, 8), :]
            column = lambda a, j: jnp.take_along_axis(a, jnp.full(a.shape, k + j, jnp.int32), axis=1)
            pivot_lanes = (lane >= k) & (lane < k + 4)
            cols = [column(tile, j) for j in range(4)]
            block = [[cols[max(i, j)][q + min(i, j) : q + min(i, j) + 1, :] for j in range(4)] for i in range(4)]
            inv = inverse_4(block)
            rows = [
                jnp.where(pivot_lanes, jnp.where(lane == k + i, 1.0, 0.0), tile[q + i : q + i + 1, :])
                for i in range(4)
            ]
            new = small_mm(inv, [[r] for r in rows])
            new = [r[0] for r in new]
            update = column(whole, 0) * new[0]
            tile_update = cols[0] * new[0]
            for i in range(1, 4):
                update = update + column(whole, i) * new[i]
                tile_update = tile_update + cols[i] * new[i]
            tile_new = jnp.where(pivot_lanes, 0.0, tile) - tile_update
            for i in range(4):
                tile_new = jnp.where(sub8 == q + i, new[i], tile_new)
            m[...] = jnp.where(pivot_lanes, 0.0, whole) - update
            m[pl.ds(r0, 8), :] = tile_new
        return carry

    lax.fori_loop(start, stop, body, 0)


def diag_of(row):
    n = row.shape[1]
    here = lax.broadcasted_iota(jnp.int32, (n, n), 0) == lax.broadcasted_iota(jnp.int32, (n, n), 1)
    return jnp.where(here, row, 0.0)


def kernel(
    leaf, imp, src, top, iop, out,
    la, lb, lc, tt, x1, x2, g3, impb, hb, opv,
    ss2, se2, ee2, h2, ss3, se3, h3,
    m1, m2, sinv, bb, xm1, xm2, v3s, v2s, sem, lsem,
):
    s = lax.axis_index("sub")
    y = lax.axis_index("src")
    c = s % 2
    x = s // 2 % 4
    z = s // 8
    beta = x % 2
    gamma = x // 2
    sib = s + 1 - 2 * c
    part2 = z * 8 + (x + 1 - 2 * beta) * 2 + c
    part3 = z * 8 + (3 - x) * 2 + c
    count = [0]
    sends = []

    def take(n):
        base = count[0]
        count[0] += n
        return base

    def push(source, dest, recv, device):
        copy = pltpu.make_async_remote_copy(
            source, dest, sem.at[take(1)], sem.at[recv], device_id=device, device_id_type=MESH
        )
        copy.start()
        sends.append(copy)

    def arrived(ref, recv):
        pltpu.make_async_remote_copy(
            ref, ref, sem.at[0], sem.at[recv], device_id=(sib, y), device_id_type=MESH
        ).wait_recv()

    class Gather:
        def __init__(self, buf):
            self.buf = buf
            self.recv = take(8)

        def start(self, source):
            mine = self.buf.at[y, c]
            for d in (1, 3, 2):
                push(source, mine, self.recv + y * 2 + c, (s, (y + d) % 4))
            push(source, mine, self.recv + y * 2 + c, (sib, y))

        def relay(self):
            for d in (1, 3, 2):
                who = (y + d) % 4
                slot = self.buf.at[who, c]
                arrived(slot, self.recv + who * 2 + c)
                push(slot, slot, self.recv + who * 2 + c, (sib, y))

        def wait(self):
            for who in range(4):
                arrived(self.buf.at[who, 1 - c], self.recv + who * 2 + 1 - c)

    class Pair:
        def __init__(self, device):
            self.device = device
            self.recv = take(1)

        def start(self, ref):
            push(ref, ref, self.recv, self.device)

        def wait(self, ref):
            arrived(ref, self.recv)

    locals_ = []

    def fetch(source, dest):
        copy = pltpu.make_async_copy(source, dest, lsem.at[len(locals_)])
        copy.start()
        locals_.append(copy)

    fetch(leaf.at[0, pl.ds(256, 128), :], la.at[y, c])
    fetch(leaf.at[0, pl.ds(384, 128), :], lb.at[y, c])
    fetch(leaf.at[0, pl.ds(0, 256), :], lc.at[y, c])
    fetch(src.at[0, :, pl.ds(pl.multiple_of(c * 128, 128), 128)], hb.at[c])
    fetch(imp, impb.at[c])
    fetch(top.at[z, pl.ds(0, 256), :], tt.at[y, 0])
    fetch(top.at[z, pl.ds(256, 256), :], tt.at[y, 1])
    fetch(iop.at[0], opv)

    barrier = pltpu.get_barrier_semaphore()
    greet = [(s, (y + d) % 4) for d in (1, 2, 3)] + [(sib, y), (part2, y), (part3, y)]
    for device in greet:
        pl.semaphore_signal(barrier, inc=1, device_id=device, device_id_type=MESH)
    pl.semaphore_wait(barrier, len(greet))

    ga, gb, gc = Gather(la), Gather(lb), Gather(lc)
    gt, gx1, gx2, gg3 = Gather(tt), Gather(x1), Gather(x2), Gather(g3)
    pimp, phb = Pair((sib, y)), Pair((sib, y))
    ga.start(leaf.at[0, pl.ds(256, 128), :])
    push(imp, impb.at[c], pimp.recv, (sib, y))
    gb.start(leaf.at[0, pl.ds(384, 128), :])
    push(
        src.at[0, :, pl.ds(pl.multiple_of((1 - c) * 128, 128), 128)], hb.at[c], phb.recv, (sib, y)
    )
    gc.start(leaf.at[0, pl.ds(0, 256), :])
    for copy in locals_:
        copy.wait()
    ga.relay()
    pimp.wait(impb.at[1 - c])
    ga.wait()

    def eliminate(s11, s12, s22, mid1, mid2, mid3):
        m1[...] = s11
        invert_tiles(m1, 0, 8)
        mid1()
        invert_tiles(m1, 8, 16)
        mid2()
        i11 = m1[...]
        b12 = s12()
        w = mm(i11, b12)
        m2[...] = s22() - mm(b12, w, TN)
        invert_tiles(m2, 0, 8)
        mid3()
        invert_tiles(m2, 8, 16)
        i22 = m2[...]
        i12 = -mm(w, i22)
        sinv[0:128, 0:128] = i11 - mm(i12, w, NT)
        sinv[0:128, 128:256] = i12
        sinv[128:256, 0:128] = i12.T
        sinv[128:256, 128:256] = i22

    ir = lambda k, lo: impb[k, 0:1, lo : lo + 128]

    def mid1():
        gb.relay()
        gt.start(tt.at[y, c])

    def mid2():
        gc.relay()
        gb.wait()

    def nothing():
        pass

    eliminate(
        la[2, 0] + la[2, 1] + diag_of(ir(0, 256) + ir(1, 256)),
        lambda: la[3, 0] + la[3, 1],
        lambda: lb[3, 0] + lb[3, 1] + diag_of(ir(0, 384) + ir(1, 384)),
        mid1, mid2, nothing,
    )
    for k in range(2):
        for q in range(2):
            col = (2 * k + q) * 128
            bb[0:128, col : col + 128] = la[q, k]
            bb[128:256, col : col + 128] = lb[q, k]
    phb.wait(hb.at[1 - c])
    bb[:, 512:640] = hb[0, 256:512, :] + hb[1, 256:512, :]
    xa = mm(sinv[...], bb[...])
    xm1[...] = xa[:, 0:512]
    x1[y, c] = xa[:, 512:640]
    gx1.start(x1.at[y, c])
    gc.wait()
    zz = mm(bb[:, 128:512], xa, TN)
    ss2[beta, 0] = lc[1, 0, 128:256, :] + diag_of(ir(0, 128)) - zz[0:128, 128:256]
    ss2[beta, 1] = -zz[0:128, 384:512]
    ss2[beta, 2] = lc[1, 1, 128:256, :] + diag_of(ir(1, 128)) - zz[256:384, 384:512]
    pss2 = [Pair((part2, y)) for _ in range(3)]
    for k in range(3):
        pss2[k].start(ss2.at[beta, k])
    se2[beta, 0, 0:128, :] = lc[0, 0, 128:256, :] - zz[0:128, 0:128]
    se2[beta, 0, 128:256, :] = -zz[256:384, 0:128]
    se2[beta, 1, 0:128, :] = -zz[0:128, 256:384]
    se2[beta, 1, 128:256, :] = lc[0, 1, 128:256, :] - zz[256:384, 256:384]
    ee2[beta, 0] = -zz[128:256, 0:128]
    ee2[beta, 1] = lc[0, 1, 0:128, :] + diag_of(ir(1, 0)) - zz[128:256, 256:384]
    h2[beta, 0:128, :] = hb[0, 128:256, :] - zz[0:128, 512:640]
    h2[beta, 128:256, :] = hb[1, 128:256, :] - zz[256:384, 512:640]
    h2[beta, 256:384, :] = hb[1, 0:128, :] - zz[128:256, 512:640]
    pse2, pee2, ph2 = Pair((part2, y)), Pair((part2, y)), Pair((part2, y))
    rse2, ree2 = Pair((sib, y)), Pair((sib, y))
    pse2.start(se2.at[beta, c])
    pee2.start(ee2.at[beta, c])
    ph2.start(h2.at[beta])

    other = 1 - beta

    def mid1():
        gt.relay()

    def mid2():
        pss2[1].wait(ss2.at[other, 1])
        pss2[2].wait(ss2.at[other, 2])

    def mid3():
        pse2.wait(se2.at[other, c])
        rse2.start(se2.at[other, c])
        pee2.wait(ee2.at[other, c])
        ree2.start(ee2.at[other, c])

    pss2[0].wait(ss2.at[other, 0])
    eliminate(
        ss2[0, 0] + ss2[1, 0], lambda: ss2[0, 1] + ss2[1, 1], lambda: ss2[0, 2] + ss2[1, 2], mid1, mid2, mid3
    )
    rse2.wait(se2.at[other, 1 - c])
    ph2.wait(h2.at[other])
    for k in range(2):
        for q in range(2):
            col = (2 * k + q) * 128
            bb[:, col : col + 128] = se2[k, q]
    bb[:, 512:640] = h2[0, 0:256, :] + h2[1, 0:256, :]
    xb = mm(sinv[...], bb[...])
    xm2[...] = xb[:, 0:512]
    x2[y, c] = xb[:, 512:640]
    ree2.wait(ee2.at[other, 1 - c])
    za = mm(bb[:, 128:256], xb, TN)
    zb = mm(bb[:, 384:512], xb, TN)
    ss3[gamma, 0] = ee2[0, 1] - za[:, 128:256]
    ss3[gamma, 1] = -za[:, 384:512]
    ss3[gamma, 2] = ee2[1, 1] - zb[:, 384:512]
    pss3 = [Pair((part3, y)) for _ in range(3)]
    pse3, ph3 = Pair((part3, y)), Pair((part3, y))
    rse3 = Pair((sib, y))
    pss3[0].start(ss3.at[gamma, 0])
    h3[gamma, 0:128, :] = h2[0, 256:384, :] - za[:, 512:640]
    h3[gamma, 128:256, :] = h2[1, 256:384, :] - zb[:, 512:640]
    ph3.start(h3.at[gamma])
    pss3[1].start(ss3.at[gamma, 1])
    pss3[2].start(ss3.at[gamma, 2])
    se3[gamma, 0, 0:128, :] = ee2[0, 0] - za[:, 0:128]
    se3[gamma, 0, 128:256, :] = -zb[:, 0:128]
    se3[gamma, 1, 0:128, :] = -za[:, 256:384]
    se3[gamma, 1, 128:256, :] = ee2[1, 0] - zb[:, 256:384]
    pse3.start(se3.at[gamma, c])
    gx2.start(x2.at[y, c])

    across = 1 - gamma

    def mid1():
        gx1.relay()
        ph3.wait(h3.at[across])
        g3[y, c] = h3[0] + h3[1]
        gg3.start(g3.at[y, c])

    def mid2():
        pss3[1].wait(ss3.at[across, 1])
        pss3[2].wait(ss3.at[across, 2])

    def mid3():
        pse3.wait(se3.at[across, c])
        rse3.start(se3.at[across, c])
        gx2.relay()

    pss3[0].wait(ss3.at[across, 0])
    eliminate(
        ss3[0, 0] + ss3[1, 0], lambda: ss3[0, 1] + ss3[1, 1], lambda: ss3[0, 2] + ss3[1, 2], mid1, mid2, mid3
    )
    gg3.relay()
    rse3.wait(se3.at[across, 1 - c])
    gt.wait()
    gx1.wait()
    gx2.wait()
    gg3.wait()

    def descend(who, carry):
        piece = lambda h, q: tt[who, h, pl.ds(pl.multiple_of(q * 128, 128), 128), :]
        lanes = lambda buf: jnp.concatenate([buf[who, 0], buf[who, 1]], axis=1)
        r = lanes(g3)
        r = r + mm(se3[0, 0], tt[who, 0, 0:128, :]) + mm(se3[0, 1], tt[who, 1, 0:128, :])
        r = r + mm(se3[1, 0], tt[who, 0, 128:256, :]) + mm(se3[1, 1], tt[who, 1, 128:256, :])
        v3 = -mm(sinv[...], r)
        v3s[...] = v3
        w2 = jnp.concatenate([piece(0, gamma), v3[0:128], piece(1, gamma), v3[128:256]], axis=0)
        v2 = -(mm(xm2[...], w2) + lanes(x2))
        v2s[...] = v2
        outer = tt[who, beta, pl.ds(pl.multiple_of(gamma * 128, 128), 128), :]
        inner = v3s[pl.ds(pl.multiple_of(beta * 128, 128), 128), :]
        w1 = jnp.concatenate([outer, v2[0:128], inner, v2[128:256]], axis=0)
        v1 = -(mm(xm1[...], w1) + lanes(x1))
        first = jnp.where(c == 0, outer, inner)
        second = v2s[pl.ds(pl.multiple_of(c * 128, 128), 128), :]
        trace = jnp.concatenate([first, second, v1], axis=0)
        out[0, :, pl.ds(pl.multiple_of(who * 256, 256), 256)] = mm(opv[...], trace)
        return carry

    lax.fori_loop(0, 4, descend, 0)
    for copy in sends:
        copy.wait_send()
    assert count[0] <= NSEM


def on_device(leaf_maps, impedance, sources, top_trace, interior_op):
    anywhere = pl.BlockSpec(memory_space=pl.ANY)
    vm = lambda *shape: pltpu.VMEM(shape, F32)
    return pl.pallas_call(
        kernel,
        out_shape=jax.ShapeDtypeStruct((1, 256, 1024), F32),
        in_specs=[anywhere] * 5,
        out_specs=pl.BlockSpec(memory_space=pltpu.VMEM),
        scratch_shapes=[
            vm(4, 2, 128, 128), vm(4, 2, 128, 128), vm(4, 2, 256, 128), vm(4, 2, 256, 256),
            vm(4, 2, 256, 128), vm(4, 2, 256, 128), vm(4, 2, 256, 128),
            vm(2, 1, 512), vm(2, 512, 128), vm(256, 512),
            vm(2, 3, 128, 128), vm(2, 2, 256, 128), vm(2, 2, 128, 128), vm(2, 384, 128),
            vm(2, 3, 128, 128), vm(2, 2, 256, 128), vm(2, 256, 128),
            vm(128, 128), vm(128, 128), vm(256, 256), vm(256, 640), vm(256, 512), vm(256, 512),
            vm(256, 256), vm(256, 256),
            pltpu.SemaphoreType.DMA((NSEM,)), pltpu.SemaphoreType.DMA((8,)),
        ],
        compiler_params=pltpu.CompilerParams(
            collective_id=0, has_side_effects=True, vmem_limit_bytes=48 * 2**20
        ),
        name="merge_solve",
    )(leaf_maps, impedance, sources, top_trace, interior_op)


def solution(mesh):
    return jax.shard_map(
        on_device,
        mesh=mesh,
        in_specs=(
            P("sub", None, "src"),
            P("sub", None),
            P("sub", None, "src"),
            P(None, None, "src"),
            P("sub", "src", None),
        ),
        out_specs=P("sub", "src", None),
        check_vma=False,
    )
```

```python
import jax
import jax.numpy as jnp
from jax import lax
from jax.experimental import pallas as pl
from jax.experimental.pallas import tpu as pltpu
from jax.sharding import PartitionSpec as P

F32 = jnp.float32
MESH = pl.DeviceIdType.MESH
NN = ((1,), (0,))
TN = ((0,), (0,))
NT = ((1,), (1,))
NSEM = 256


def mm(a, b, dims=NN):
    return lax.dot_general(
        a, b, (dims, ((), ())), precision=lax.Precision.HIGHEST, preferred_element_type=F32
    )


def split(a):
    high = a.astype(jnp.bfloat16)
    return high, (a - high.astype(F32)).astype(jnp.bfloat16)


def mm3(a, b):
    dot = lambda p, q: lax.dot_general(p, q, (NN, ((), ())), preferred_element_type=F32)
    return dot(a[0], b[0]) + (dot(a[0], b[1]) + dot(a[1], b[0]))


def tile_steps(panel, at, k):
    lane = lax.broadcasted_iota(jnp.int32, (8, 128), 1)
    row = lax.broadcasted_iota(jnp.int32, (8, 128), 0)
    column = lambda v, j: jnp.take_along_axis(v, jnp.full(v.shape, k + j, jnp.int32), axis=1)
    spread = lambda v, i: jnp.broadcast_to(v[i : i + 1, :], (8, 128))
    tile = panel[at]
    cols = [column(tile, j) for j in range(8)]
    others = {u: [column(panel[u], j) for j in range(8)] for u in range(len(panel)) if u != at}
    for q in range(0, 8, 2):
        a, b, d = spread(cols[q], q), spread(cols[q + 1], q), spread(cols[q + 1], q + 1)
        r = 1.0 / (a * d - b * b)
        i00, i01, i11 = d * r, -(b * r), a * r
        pivots = (row >= q) & (row < q + 2)
        m0 = jnp.where(pivots, jnp.where(row == q, -1.0, 0.0), cols[q])
        m1 = jnp.where(pivots, jnp.where(row == q + 1, -1.0, 0.0), cols[q + 1])

        def change(t0, t1):
            return m0 * (i00 * t0 + i01 * t1) + m1 * (i01 * t0 + i11 * t1)

        for j in range(q + 2, 8):
            cols[j] = jnp.where(pivots, 0.0, cols[j]) - change(spread(cols[j], q), spread(cols[j], q + 1))
        l0, l1 = lane == k + q, lane == k + q + 1
        t0 = jnp.where(l0, 1.0, jnp.where(l1, 0.0, spread(tile, q)))
        t1 = jnp.where(l1, 1.0, jnp.where(l0, 0.0, spread(tile, q + 1)))
        tile = jnp.where(pivots | l0 | l1, 0.0, tile) - change(t0, t1)
    rows = [spread(tile, j) for j in range(8)]
    done = (lane >= k) & (lane < k + 8)

    def follow(u):
        terms = [x * r for x, r in zip(others[u], rows)]
        while len(terms) > 1:
            terms = [terms[i] + terms[i + 1] for i in range(0, len(terms), 2)]
        return jnp.where(done, 0.0, panel[u]) - terms[0]

    return [tile if u == at else follow(u) for u in range(len(panel))]


PANEL = 64


def invert_panels(m, start, stop):
    n = m.shape[0]
    lane = lax.broadcasted_iota(jnp.int32, (n, n), 1)

    def body(t, carry):
        r0 = pl.multiple_of(t * PANEL, PANEL)
        whole = m[...]
        tiles = [pl.ds(pl.multiple_of(r0 + 8 * i, 8), 8) for i in range(PANEL // 8)]
        panel = [m[i, :] for i in tiles]
        for at in range(PANEL // 8):
            panel = tile_steps(panel, at, r0 + 8 * at)
        inside = (lane >= r0) & (lane < r0 + PANEL)
        rows = jnp.concatenate(panel * (n // PANEL), axis=0)
        m[...] = jnp.where(inside, 0.0, whole) - mm(jnp.where(inside, whole, 0.0), rows)
        for i, tile in zip(tiles, panel):
            m[i, :] = tile
        return carry

    lax.fori_loop(start, stop, body, 0)


def diag_of(row):
    n = row.shape[1]
    here = lax.broadcasted_iota(jnp.int32, (n, n), 0) == lax.broadcasted_iota(jnp.int32, (n, n), 1)
    return jnp.where(here, row, 0.0)


def kernel(
    leaf, imp, src, top, iop, out,
    la, lb, lc, tt, x1, x2, g3, impb, hb, opv,
    ss2, se2, ee2, h2, ss3, se3, h3,
    m1, m2, sinv, bb, xm1, xm2, k1s, kv2, kt, k3, rs, sem, lsem,
):
    s = lax.axis_index("sub")
    y = lax.axis_index("src")
    c = s % 2
    x = s // 2 % 4
    z = s // 8
    beta = x % 2
    gamma = x // 2
    sib = s + 1 - 2 * c
    part2 = z * 8 + (x + 1 - 2 * beta) * 2 + c
    part3 = z * 8 + (3 - x) * 2 + c
    count = [0]
    sends = []

    def take(n):
        base = count[0]
        count[0] += n
        return base

    def push(source, dest, recv, device):
        copy = pltpu.make_async_remote_copy(
            source, dest, sem.at[take(1)], sem.at[recv], device_id=device, device_id_type=MESH
        )
        copy.start()
        sends.append(copy)

    def arrived(ref, recv):
        pltpu.make_async_remote_copy(
            ref, ref, sem.at[0], sem.at[recv], device_id=(sib, y), device_id_type=MESH
        ).wait_recv()

    class Gather:
        def __init__(self, buf):
            self.buf = buf
            self.recv = take(8)

        def start(self, source):
            mine = self.buf.at[y, c]
            for d in (1, 3, 2):
                push(source, mine, self.recv + y * 2 + c, (s, (y + d) % 4))
            push(source, mine, self.recv + y * 2 + c, (sib, y))

        def relay(self):
            for d in (1, 3, 2):
                who = (y + d) % 4
                slot = self.buf.at[who, c]
                arrived(slot, self.recv + who * 2 + c)
                push(slot, slot, self.recv + who * 2 + c, (sib, y))

        def wait(self):
            for who in range(4):
                arrived(self.buf.at[who, 1 - c], self.recv + who * 2 + 1 - c)

    class Pair:
        def __init__(self, device):
            self.device = device
            self.recv = take(1)

        def start(self, ref):
            push(ref, ref, self.recv, self.device)

        def wait(self, ref):
            arrived(ref, self.recv)

    locals_ = []

    def fetch(source, dest):
        copy = pltpu.make_async_copy(source, dest, lsem.at[len(locals_)])
        copy.start()
        locals_.append(copy)

    fetch(leaf.at[0, pl.ds(256, 128), :], la.at[y, c])
    fetch(leaf.at[0, pl.ds(384, 128), :], lb.at[y, c])
    fetch(leaf.at[0, pl.ds(0, 256), :], lc.at[y, c])
    fetch(src.at[0, :, pl.ds(pl.multiple_of(c * 128, 128), 128)], hb.at[c])
    fetch(imp, impb.at[c])
    fetch(top.at[z, pl.ds(0, 256), :], tt.at[y, 0])
    fetch(top.at[z, pl.ds(256, 256), :], tt.at[y, 1])
    fetch(iop.at[0], opv)

    barrier = pltpu.get_barrier_semaphore()
    greet = [(s, (y + d) % 4) for d in (1, 2, 3)] + [(sib, y), (part2, y), (part3, y)]
    for device in greet:
        pl.semaphore_signal(barrier, inc=1, device_id=device, device_id_type=MESH)
    pl.semaphore_wait(barrier, len(greet))

    ga, gb, gc = Gather(la), Gather(lb), Gather(lc)
    gt, gx1, gx2, gg3 = Gather(tt), Gather(x1), Gather(x2), Gather(g3)
    pimp, phb = Pair((sib, y)), Pair((sib, y))
    ga.start(leaf.at[0, pl.ds(256, 128), :])
    push(imp, impb.at[c], pimp.recv, (sib, y))
    gb.start(leaf.at[0, pl.ds(384, 128), :])
    push(
        src.at[0, :, pl.ds(pl.multiple_of((1 - c) * 128, 128), 128)], hb.at[c], phb.recv, (sib, y)
    )
    gc.start(leaf.at[0, pl.ds(0, 256), :])
    for copy in locals_:
        copy.wait()
    ga.relay()
    pimp.wait(impb.at[1 - c])
    ga.wait()

    def eliminate(s11, s12, s22, mid1, mid2, mid3, mid4):
        m1[...] = s11
        invert_panels(m1, 0, 1)
        mid1()
        invert_panels(m1, 1, 2)
        mid2()
        i11 = m1[...]
        b12 = s12()
        w = mm(i11, b12)
        m2[...] = s22() - mm(b12, w, TN)
        invert_panels(m2, 0, 1)
        mid3()
        invert_panels(m2, 1, 2)
        mid4()
        i22 = m2[...]
        i12 = -mm(w, i22)
        sinv[0:128, 0:128] = i11 - mm(i12, w, NT)
        sinv[0:128, 128:256] = i12
        sinv[128:256, 0:128] = i12.T
        sinv[128:256, 128:256] = i22

    ir = lambda k, lo: impb[k, 0:1, lo : lo + 128]

    def mid1():
        gb.relay()
        gt.start(tt.at[y, c])

    def mid2():
        gc.relay()
        gb.wait()

    def nothing():
        pass

    eliminate(
        la[2, 0] + la[2, 1] + diag_of(ir(0, 256) + ir(1, 256)),
        lambda: la[3, 0] + la[3, 1],
        lambda: lb[3, 0] + lb[3, 1] + diag_of(ir(0, 384) + ir(1, 384)),
        mid1, mid2, nothing, nothing,
    )
    for k in range(2):
        for q in range(2):
            col = (2 * k + q) * 128
            bb[0:128, col : col + 128] = la[q, k]
            bb[128:256, col : col + 128] = lb[q, k]
    phb.wait(hb.at[1 - c])
    bb[:, 512:640] = hb[0, 256:512, :] + hb[1, 256:512, :]
    xa = mm(sinv[...], bb[...])
    xm1[...] = xa[:, 0:512]
    x1[y, c] = xa[:, 512:640]
    gx1.start(x1.at[y, c])
    gc.wait()
    zz = mm(bb[:, 128:512], xa, TN)
    ss2[beta, 0] = lc[1, 0, 128:256, :] + diag_of(ir(0, 128)) - zz[0:128, 128:256]
    ss2[beta, 1] = -zz[0:128, 384:512]
    ss2[beta, 2] = lc[1, 1, 128:256, :] + diag_of(ir(1, 128)) - zz[256:384, 384:512]
    pss2 = [Pair((part2, y)) for _ in range(3)]
    for k in range(3):
        pss2[k].start(ss2.at[beta, k])
    se2[beta, 0, 0:128, :] = lc[0, 0, 128:256, :] - zz[0:128, 0:128]
    se2[beta, 0, 128:256, :] = -zz[256:384, 0:128]
    se2[beta, 1, 0:128, :] = -zz[0:128, 256:384]
    se2[beta, 1, 128:256, :] = lc[0, 1, 128:256, :] - zz[256:384, 256:384]
    ee2[beta, 0] = -zz[128:256, 0:128]
    ee2[beta, 1] = lc[0, 1, 0:128, :] + diag_of(ir(1, 0)) - zz[128:256, 256:384]
    h2[beta, 0:128, :] = hb[0, 128:256, :] - zz[0:128, 512:640]
    h2[beta, 128:256, :] = hb[1, 128:256, :] - zz[256:384, 512:640]
    h2[beta, 256:384, :] = hb[1, 0:128, :] - zz[128:256, 512:640]
    pse2, pee2, ph2 = Pair((part2, y)), Pair((part2, y)), Pair((part2, y))
    rse2, ree2 = Pair((sib, y)), Pair((sib, y))
    pse2.start(se2.at[beta, c])
    pee2.start(ee2.at[beta, c])
    ph2.start(h2.at[beta])

    op_s = split(opv[:, 256:512])
    k1 = -mm3(op_s, split(xm1[...]))
    e0, e1 = opv[:, 0:128], opv[:, 128:256]
    zero = jnp.zeros_like(e0)
    pick = lambda cond, v: jnp.where(cond, v, zero)
    k1s[:, 0:128] = k1[:, 0:128] + pick(c == 0, e0)
    k1s[:, 128:256] = k1[:, 256:384] + pick(c == 1, e0)
    kv2[:, 0:128] = k1[:, 128:256] + pick(c == 0, e1)
    kv2[:, 128:256] = k1[:, 384:512] + pick(c == 1, e1)

    other = 1 - beta

    def mid1():
        gt.relay()

    def mid2():
        pss2[1].wait(ss2.at[other, 1])
        pss2[2].wait(ss2.at[other, 2])

    def mid3():
        pse2.wait(se2.at[other, c])
        rse2.start(se2.at[other, c])
        pee2.wait(ee2.at[other, c])
        ree2.start(ee2.at[other, c])

    pss2[0].wait(ss2.at[other, 0])
    eliminate(
        ss2[0, 0] + ss2[1, 0], lambda: ss2[0, 1] + ss2[1, 1], lambda: ss2[0, 2] + ss2[1, 2],
        mid1, mid2, mid3, gx1.relay,
    )
    rse2.wait(se2.at[other, 1 - c])
    ph2.wait(h2.at[other])
    for k in range(2):
        for q in range(2):
            col = (2 * k + q) * 128
            bb[:, col : col + 128] = se2[k, q]
    bb[:, 512:640] = h2[0, 0:256, :] + h2[1, 0:256, :]
    xb = mm(sinv[...], bb[...])
    xm2[...] = xb[:, 0:512]
    x2[y, c] = xb[:, 512:640]
    ree2.wait(ee2.at[other, 1 - c])
    za = mm(bb[:, 128:256], xb, TN)
    zb = mm(bb[:, 384:512], xb, TN)
    ss3[gamma, 0] = ee2[0, 1] - za[:, 128:256]
    ss3[gamma, 1] = -za[:, 384:512]
    ss3[gamma, 2] = ee2[1, 1] - zb[:, 384:512]
    pss3 = [Pair((part3, y)) for _ in range(3)]
    pse3, ph3 = Pair((part3, y)), Pair((part3, y))
    rse3 = Pair((sib, y))
    pss3[0].start(ss3.at[gamma, 0])
    h3[gamma, 0:128, :] = h2[0, 256:384, :] - za[:, 512:640]
    h3[gamma, 128:256, :] = h2[1, 256:384, :] - zb[:, 512:640]
    ph3.start(h3.at[gamma])
    pss3[1].start(ss3.at[gamma, 1])
    pss3[2].start(ss3.at[gamma, 2])
    se3[gamma, 0, 0:128, :] = ee2[0, 0] - za[:, 0:128]
    se3[gamma, 0, 128:256, :] = -zb[:, 0:128]
    se3[gamma, 1, 0:128, :] = -za[:, 256:384]
    se3[gamma, 1, 128:256, :] = ee2[1, 0] - zb[:, 256:384]
    pse3.start(se3.at[gamma, c])
    gx2.start(x2.at[y, c])

    kb = -mm3(split(kv2[...]), split(xm2[...]))
    ko, ki = k1s[:, 0:128], k1s[:, 128:256]
    kt[:, 0:128] = kb[:, 0:128] + pick(beta == 0, ko)
    kt[:, 128:256] = kb[:, 256:384] + pick(beta == 1, ko)
    k3[:, 0:128] = kb[:, 128:256] + pick(beta == 0, ki)
    k3[:, 128:256] = kb[:, 384:512] + pick(beta == 1, ki)
    gt.wait()
    gx1.wait()
    chunk = lambda who: pl.ds(pl.multiple_of(who * 256, 256), 256)
    lanes = lambda buf, who: jnp.concatenate([buf[who, 0], buf[who, 1]], axis=1)
    quarter = pl.ds(pl.multiple_of(gamma * 128, 128), 128)

    def known(who, carry):
        outer = jnp.concatenate([tt[who, 0, quarter, :], tt[who, 1, quarter, :]], axis=0)
        out[0, :, chunk(who)] = mm3(split(kt[...]), split(outer)) - mm3(
            split(opv[:, 256:512]), split(lanes(x1, who))
        )
        return carry

    lax.fori_loop(0, 4, known, 0)

    across = 1 - gamma

    def mid1():
        ph3.wait(h3.at[across])
        g3[y, c] = h3[0] + h3[1]
        gg3.start(g3.at[y, c])

    def mid2():
        pss3[1].wait(ss3.at[across, 1])
        pss3[2].wait(ss3.at[across, 2])

    def mid3():
        pse3.wait(se3.at[across, c])
        rse3.start(se3.at[across, c])
        gx2.relay()

    pss3[0].wait(ss3.at[across, 0])
    eliminate(
        ss3[0, 0] + ss3[1, 0], lambda: ss3[0, 1] + ss3[1, 1], lambda: ss3[0, 2] + ss3[1, 2],
        mid1, mid2, mid3, gg3.relay,
    )
    rse3.wait(se3.at[across, 1 - c])
    gx2.wait()
    for k in range(2):
        for q in range(2):
            col = (2 * q + k) * 128
            bb[:, col : col + 128] = se3[k, q]

    def right_side(who, carry):
        whole = jnp.concatenate([tt[who, 0], tt[who, 1]], axis=0)
        rs[:, chunk(who)] = mm3(split(bb[:, 0:512]), split(whole))
        out[0, :, chunk(who)] -= mm3(split(kv2[...]), split(lanes(x2, who)))
        return carry

    lax.fori_loop(0, 4, right_side, 0)
    k3[...] = -mm3(split(k3[...]), split(sinv[...]))
    gg3.wait()

    def finish(who, carry):
        out[0, :, chunk(who)] += mm3(split(k3[...]), split(rs[:, chunk(who)] + lanes(g3, who)))
        return carry

    lax.fori_loop(0, 4, finish, 0)
    for copy in sends:
        copy.wait_send()
    assert count[0] <= NSEM


def on_device(leaf_maps, impedance, sources, top_trace, interior_op):
    anywhere = pl.BlockSpec(memory_space=pltpu.HBM)
    vm = lambda *shape: pltpu.VMEM(shape, F32)
    return pl.pallas_call(
        kernel,
        out_shape=jax.ShapeDtypeStruct((1, 256, 1024), F32),
        in_specs=[anywhere] * 5,
        out_specs=pl.BlockSpec(memory_space=pltpu.VMEM),
        scratch_shapes=[
            vm(4, 2, 128, 128), vm(4, 2, 128, 128), vm(4, 2, 256, 128), vm(4, 2, 256, 256),
            vm(4, 2, 256, 128), vm(4, 2, 256, 128), vm(4, 2, 256, 128),
            vm(2, 1, 512), vm(2, 512, 128), vm(256, 512),
            vm(2, 3, 128, 128), vm(2, 2, 256, 128), vm(2, 2, 128, 128), vm(2, 384, 128),
            vm(2, 3, 128, 128), vm(2, 2, 256, 128), vm(2, 256, 128),
            vm(128, 128), vm(128, 128), vm(256, 256), vm(256, 640), vm(256, 512), vm(256, 512),
            vm(256, 256), vm(256, 256), vm(256, 256), vm(256, 256), vm(256, 1024),
            pltpu.SemaphoreType.DMA((NSEM,)), pltpu.SemaphoreType.DMA((8,)),
        ],
        compiler_params=pltpu.CompilerParams(
            collective_id=0, has_side_effects=True, vmem_limit_bytes=48 * 2**20
        ),
        name="merge_solve",
    )(leaf_maps, impedance, sources, top_trace, interior_op)


def solution(mesh):
    return jax.shard_map(
        on_device,
        mesh=mesh,
        in_specs=(
            P("sub", None, "src"),
            P("sub", None),
            P("sub", None, "src"),
            P(None, None, "src"),
            P("sub", "src", None),
        ),
        out_specs=P("sub", "src", None),
        check_vma=False,
    )
```

```python
import jax
import jax.numpy as jnp
from jax import lax
from jax.experimental import pallas as pl
from jax.experimental.pallas import tpu as pltpu
from jax.sharding import PartitionSpec as P

F32 = jnp.float32
MESH = pl.DeviceIdType.MESH
NN = ((1,), (0,))
TN = ((0,), (0,))
NT = ((1,), (1,))
NSEM = 256


def mm(a, b, dims=NN):
    return lax.dot_general(
        a, b, (dims, ((), ())), precision=lax.Precision.HIGHEST, preferred_element_type=F32
    )


def split(a):
    high = a.astype(jnp.bfloat16)
    return high, (a - high.astype(F32)).astype(jnp.bfloat16)


def mm3(a, b):
    dot = lambda p, q: lax.dot_general(p, q, (NN, ((), ())), preferred_element_type=F32)
    return dot(a[0], b[0]) + (dot(a[0], b[1]) + dot(a[1], b[0]))


def tile_steps(panel, at, k):
    lane = lax.broadcasted_iota(jnp.int32, (8, 128), 1)
    row = lax.broadcasted_iota(jnp.int32, (8, 128), 0)
    column = lambda v, j: jnp.take_along_axis(v, jnp.full(v.shape, k + j, jnp.int32), axis=1)
    spread = lambda v, i: jnp.broadcast_to(v[i : i + 1, :], (8, 128))
    tile = panel[at]
    cols = [column(tile, j) for j in range(8)]
    others = {u: [column(panel[u], j) for j in range(8)] for u in range(len(panel)) if u != at}
    for q in range(0, 8, 2):
        a, b, d = spread(cols[q], q), spread(cols[q + 1], q), spread(cols[q + 1], q + 1)
        r = 1.0 / (a * d - b * b)
        i00, i01, i11 = d * r, -(b * r), a * r
        pivots = (row >= q) & (row < q + 2)
        m0 = jnp.where(pivots, jnp.where(row == q, -1.0, 0.0), cols[q])
        m1 = jnp.where(pivots, jnp.where(row == q + 1, -1.0, 0.0), cols[q + 1])

        def change(t0, t1):
            return m0 * (i00 * t0 + i01 * t1) + m1 * (i01 * t0 + i11 * t1)

        for j in range(q + 2, 8):
            cols[j] = jnp.where(pivots, 0.0, cols[j]) - change(spread(cols[j], q), spread(cols[j], q + 1))
        l0, l1 = lane == k + q, lane == k + q + 1
        t0 = jnp.where(l0, 1.0, jnp.where(l1, 0.0, spread(tile, q)))
        t1 = jnp.where(l1, 1.0, jnp.where(l0, 0.0, spread(tile, q + 1)))
        tile = jnp.where(pivots | l0 | l1, 0.0, tile) - change(t0, t1)
    rows = [spread(tile, j) for j in range(8)]
    done = (lane >= k) & (lane < k + 8)

    def follow(u):
        terms = [x * r for x, r in zip(others[u], rows)]
        while len(terms) > 1:
            terms = [terms[i] + terms[i + 1] for i in range(0, len(terms), 2)]
        return jnp.where(done, 0.0, panel[u]) - terms[0]

    return [tile if u == at else follow(u) for u in range(len(panel))]


PANEL = 64


def invert_panels(m, start, stop):
    n = m.shape[0]
    lane = lax.broadcasted_iota(jnp.int32, (n, n), 1)

    def body(t, carry):
        r0 = pl.multiple_of(t * PANEL, PANEL)
        whole = m[...]
        tiles = [pl.ds(pl.multiple_of(r0 + 8 * i, 8), 8) for i in range(PANEL // 8)]
        panel = [m[i, :] for i in tiles]
        for at in range(PANEL // 8):
            panel = tile_steps(panel, at, r0 + 8 * at)
        inside = (lane >= r0) & (lane < r0 + PANEL)
        rows = jnp.concatenate(panel * (n // PANEL), axis=0)
        m[...] = jnp.where(inside, 0.0, whole) - mm(jnp.where(inside, whole, 0.0), rows)
        for i, tile in zip(tiles, panel):
            m[i, :] = tile
        return carry

    lax.fori_loop(start, stop, body, 0)


def diag_of(row):
    n = row.shape[1]
    here = lax.broadcasted_iota(jnp.int32, (n, n), 0) == lax.broadcasted_iota(jnp.int32, (n, n), 1)
    return jnp.where(here, row, 0.0)


def kernel(
    leaf, imp, src, top, iop, out,
    s11, s12, s22, bq, e0, e1, tt, x1, x2, g3, impb, hb, town, opv,
    ss2, se2, ee2, h2, ss3, h3,
    m1, m2, sinv, bb, xm2, k1s, kv2, kt, k3, sem, lsem,
):
    s = lax.axis_index("sub")
    y = lax.axis_index("src")
    c = s % 2
    x = s // 2 % 4
    z = s // 8
    beta = x % 2
    gamma = x // 2
    sib = s + 1 - 2 * c
    part2 = z * 8 + (x + 1 - 2 * beta) * 2 + c
    part3 = z * 8 + (3 - x) * 2 + c

    barrier = pltpu.get_barrier_semaphore()
    greet = [(s, (y + d) % 4) for d in (1, 2, 3)] + [(sib, y), (part2, y), (part3, y)]
    for device in greet:
        pl.semaphore_signal(barrier, inc=1, device_id=device, device_id_type=MESH)

    count = [0]
    sends = []

    def take(n):
        base = count[0]
        count[0] += n
        return base

    def push(source, dest, recv, device, cond=None):
        sent = take(1)

        def make():
            return pltpu.make_async_remote_copy(
                source, dest, sem.at[sent], sem.at[recv], device_id=device, device_id_type=MESH
            )

        make().start()
        sends.append((cond, make))

    def arrived(ref, recv):
        pltpu.make_async_remote_copy(
            ref, ref, sem.at[0], sem.at[recv], device_id=(sib, y), device_id_type=MESH
        ).wait_recv()

    class Gather:
        def __init__(self, buf):
            self.buf = buf
            self.recv = take(8)

        def start(self):
            mine = self.buf.at[y, c]
            for d in (1, 3, 2):
                push(mine, mine, self.recv + y * 2 + c, (s, (y + d) % 4))
            push(mine, mine, self.recv + y * 2 + c, (sib, y))

        def relay(self):
            for d in (1, 3, 2):
                who = (y + d) % 4
                slot = self.buf.at[who, c]
                arrived(slot, self.recv + who * 2 + c)
                push(slot, slot, self.recv + who * 2 + c, (sib, y))

        def wait(self):
            for who in range(4):
                arrived(self.buf.at[who, 1 - c], self.recv + who * 2 + 1 - c)

    class Spread:
        def __init__(self, owner, source, buf):
            self.owner, self.source, self.buf = owner, source, buf
            self.recv = take(2)
            self.local = pltpu.make_async_copy(source, buf.at[c], lsem.at[take_local()])

        def start(self):
            mine = self.buf.at[c]

            @pl.when(y == self.owner)
            def _():
                self.local.start()
                for d in (1, 3, 2):
                    push(self.source, mine, self.recv, (s, (self.owner + d) % 4), True)
                push(self.source, mine, self.recv + 1, (sib, y), True)

            for i in range(len(sends) - 4, len(sends)):
                sends[i] = (y == self.owner, sends[i][1])

        def relay(self):
            mine = self.buf.at[c]

            @pl.when(y != self.owner)
            def _():
                arrived(mine, self.recv)
                push(mine, mine, self.recv + 1, (sib, y), True)

            sends[-1] = (y != self.owner, sends[-1][1])

        def wait(self):
            @pl.when(y == self.owner)
            def _():
                self.local.wait()

            arrived(self.buf.at[1 - c], self.recv + 1)

    class Pair:
        def __init__(self, device):
            self.device = device
            self.recv = take(1)

        def start(self, ref):
            push(ref, ref, self.recv, self.device)

        def wait(self, ref):
            arrived(ref, self.recv)

    locals_ = []
    local_count = [0]

    def take_local():
        local_count[0] += 1
        return local_count[0] - 1

    def fetch(source, dest):
        copy = pltpu.make_async_copy(source, dest, lsem.at[take_local()])
        copy.start()
        locals_.append(copy)

    own_lanes = pl.ds(pl.multiple_of(c * 128, 128), 128)
    rows = lambda lo, n: leaf.at[0, pl.ds(lo, n), :]
    b11, b12, b22 = Spread(2, rows(256, 128), s11), Spread(3, rows(256, 128), s12), Spread(3, rows(384, 128), s22)
    bb0, bb1 = Spread(0, rows(256, 256), bq.at[0]), Spread(1, rows(256, 256), bq.at[1])
    be0, be1 = Spread(0, rows(0, 256), e0), Spread(1, rows(128, 128), e1)
    gt, gx1, gx2, gg3 = Gather(tt), Gather(x1), Gather(x2), Gather(g3)
    pimp, phb = Pair((sib, y)), Pair((sib, y))
    fetch(imp, impb.at[c])

    pl.semaphore_wait(barrier, len(greet))
    b11.start()
    push(imp, impb.at[c], pimp.recv, (sib, y))
    b12.start()
    b22.start()
    push(src.at[0, :, pl.ds(pl.multiple_of((1 - c) * 128, 128), 128)], hb.at[c], phb.recv, (sib, y))
    fetch(src.at[0, :, own_lanes], hb.at[c])
    fetch(top.at[z, pl.ds(pl.multiple_of(c * 256 + gamma * 128, 128), 128), :], tt.at[y, c])
    for h in range(2):
        quarter = pl.ds(pl.multiple_of(h * 256 + gamma * 128, 128), 128)
        fetch(top.at[z, quarter, own_lanes], town.at[pl.ds(h * 128, 128), :])
    fetch(iop.at[0], opv)
    b11.relay()
    bb0.start()
    bb1.start()
    b11.wait()
    pimp.wait(impb.at[1 - c])
    for copy in locals_:
        copy.wait()

    def eliminate(first, off, last, mid1, mid2, mid3, mid4):
        m1[...] = first
        invert_panels(m1, 0, 1)
        mid1()
        invert_panels(m1, 1, 2)
        mid2()
        i11 = m1[...]
        side = off()
        w = mm(i11, side)
        m2[...] = last() - mm(side, w, TN)
        invert_panels(m2, 0, 1)
        mid3()
        invert_panels(m2, 1, 2)
        mid4()
        i22 = m2[...]
        i12 = -mm(w, i22)
        sinv[0:128, 0:128] = i11 - mm(i12, w, NT)
        sinv[0:128, 128:256] = i12
        sinv[128:256, 0:128] = i12.T
        sinv[128:256, 128:256] = i22

    def nothing():
        pass

    ir = lambda k, lo: impb[k, 0:1, lo : lo + 128]

    def mid1():
        b12.relay()
        b22.relay()
        be0.start()
        be1.start()

    def mid2():
        b12.wait()
        b22.wait()

    def mid3():
        bb0.relay()
        bb1.relay()
        gt.start()

    def mid4():
        be0.relay()
        be1.relay()

    eliminate(
        s11[0] + s11[1] + diag_of(ir(0, 256) + ir(1, 256)),
        lambda: s12[0] + s12[1],
        lambda: s22[0] + s22[1] + diag_of(ir(0, 384) + ir(1, 384)),
        mid1, mid2, mid3, mid4,
    )
    bb0.wait()
    bb1.wait()
    for k in range(2):
        for q in range(2):
            bb[:, (2 * k + q) * 128 : (2 * k + q + 1) * 128] = bq[q, k]
    phb.wait(hb.at[1 - c])
    bb[:, 512:640] = hb[0, 256:512, :] + hb[1, 256:512, :]
    xa = mm(sinv[...], bb[...])
    be0.wait()
    be1.wait()
    zz = mm(bb[:, 128:512], xa, TN)
    ss2[beta, 0] = e1[0] + diag_of(ir(0, 128)) - zz[0:128, 128:256]
    ss2[beta, 1] = -zz[0:128, 384:512]
    ss2[beta, 2] = e1[1] + diag_of(ir(1, 128)) - zz[256:384, 384:512]
    p20, p2s, r2s = Pair((part2, y)), Pair((part2, y)), Pair((sib, y))
    pse2, pee2, ph2a, ph2b = (Pair((part2, y)) for _ in range(4))
    rse2, ree2 = Pair((sib, y)), Pair((sib, y))
    p20.start(ss2.at[beta, 0])
    p2s.start(ss2.at[beta, 1 + c])
    se2[beta, 0, 0:128, :] = e0[0, 128:256, :] - zz[0:128, 0:128]
    se2[beta, 0, 128:256, :] = -zz[256:384, 0:128]
    se2[beta, 1, 0:128, :] = -zz[0:128, 256:384]
    se2[beta, 1, 128:256, :] = e0[1, 128:256, :] - zz[256:384, 256:384]
    pse2.start(se2.at[beta, c])
    h2[beta, 0:128, :] = hb[0, 128:256, :] - zz[0:128, 512:640]
    h2[beta, 128:256, :] = hb[1, 128:256, :] - zz[256:384, 512:640]
    h2[beta, 256:384, :] = hb[1, 0:128, :] - zz[128:256, 512:640]
    ph2a.start(h2.at[beta, pl.ds(0, 256)])
    ee2[beta, 0] = -zz[128:256, 0:128]
    ee2[beta, 1] = e0[1, 0:128, :] + diag_of(ir(1, 0)) - zz[128:256, 256:384]
    pee2.start(ee2.at[beta, c])
    ph2b.start(h2.at[beta, pl.ds(256, 128)])
    x1[y, c] = xa[:, 512:640]

    k1 = -mm3(split(opv[:, 256:512]), split(xa[:, 0:512]))
    o0, o1 = opv[:, 0:128], opv[:, 128:256]
    pick = lambda cond, v: jnp.where(cond, v, jnp.zeros_like(v))
    k1s[:, 0:128] = k1[:, 0:128] + pick(c == 0, o0)
    k1s[:, 128:256] = k1[:, 256:384] + pick(c == 1, o0)
    kv2[:, 0:128] = k1[:, 128:256] + pick(c == 0, o1)
    kv2[:, 128:256] = k1[:, 384:512] + pick(c == 1, o1)

    other = 1 - beta

    def mid1():
        p2s.wait(ss2.at[other, 1 + c])
        r2s.start(ss2.at[other, 1 + c])
        gt.relay()
        gx1.start()

    def mid2():
        r2s.wait(ss2.at[other, 2 - c])

    def mid3():
        pse2.wait(se2.at[other, c])
        rse2.start(se2.at[other, c])

    def mid4():
        pee2.wait(ee2.at[other, c])
        ree2.start(ee2.at[other, c])

    p20.wait(ss2.at[other, 0])
    eliminate(
        ss2[0, 0] + ss2[1, 0], lambda: ss2[0, 1] + ss2[1, 1], lambda: ss2[0, 2] + ss2[1, 2],
        mid1, mid2, mid3, mid4,
    )
    rse2.wait(se2.at[other, 1 - c])
    ph2a.wait(h2.at[other, pl.ds(0, 256)])
    for k in range(2):
        for q in range(2):
            col = (2 * k + q) * 128
            bb[:, col : col + 128] = se2[k, q]
    bb[:, 512:640] = h2[0, 0:256, :] + h2[1, 0:256, :]
    xb = mm(sinv[...], bb[...])
    xm2[...] = xb[:, 0:512]
    x2[y, c] = xb[:, 512:640]
    ree2.wait(ee2.at[other, 1 - c])
    za = mm(bb[:, 128:256], xb, TN)
    zb = mm(bb[:, 384:512], xb, TN)
    ss3[gamma, 0] = ee2[0, 1] - za[:, 128:256]
    ss3[gamma, 1] = -za[:, 384:512]
    ss3[gamma, 2] = ee2[1, 1] - zb[:, 384:512]
    p30, p3s, r3s, ph3 = Pair((part3, y)), Pair((part3, y)), Pair((sib, y)), Pair((part3, y))
    p30.start(ss3.at[gamma, 0])
    ph2b.wait(h2.at[other, pl.ds(256, 128)])
    t0, t1 = town[0:128, :], town[128:256, :]
    h3[gamma, 0:128, :] = (
        h2[0, 256:384, :] - za[:, 512:640] + mm(ee2[0, 0] - za[:, 0:128], t0) - mm(za[:, 256:384], t1)
    )
    h3[gamma, 128:256, :] = (
        h2[1, 256:384, :] - zb[:, 512:640] - mm(zb[:, 0:128], t0) + mm(ee2[1, 0] - zb[:, 256:384], t1)
    )
    ph3.start(h3.at[gamma])
    p3s.start(ss3.at[gamma, 1 + c])
    gx2.start()

    kb = -mm3(split(kv2[...]), split(xm2[...]))
    ko, ki = k1s[:, 0:128], k1s[:, 128:256]
    kt[:, 0:128] = kb[:, 0:128] + pick(beta == 0, ko)
    kt[:, 128:256] = kb[:, 256:384] + pick(beta == 1, ko)
    k3[:, 0:128] = kb[:, 128:256] + pick(beta == 0, ki)
    k3[:, 128:256] = kb[:, 384:512] + pick(beta == 1, ki)
    chunk = lambda who: pl.ds(pl.multiple_of(who * 256, 256), 256)
    lanes = lambda buf, who: jnp.concatenate([buf[who, 0], buf[who, 1]], axis=1)

    across = 1 - gamma

    def mid1():
        p3s.wait(ss3.at[across, 1 + c])
        r3s.start(ss3.at[across, 1 + c])
        ph3.wait(h3.at[across])
        g3[y, c] = h3[0] + h3[1]
        gg3.start()

    def mid2():
        gx1.relay()
        r3s.wait(ss3.at[across, 2 - c])

    def mid3():
        gx2.relay()

    p30.wait(ss3.at[across, 0])
    eliminate(
        ss3[0, 0] + ss3[1, 0], lambda: ss3[0, 1] + ss3[1, 1], lambda: ss3[0, 2] + ss3[1, 2],
        mid1, mid2, mid3, gg3.relay,
    )
    gt.wait()
    gx1.wait()

    def known(who, carry):
        outer = jnp.concatenate([tt[who, 0], tt[who, 1]], axis=0)
        out[0, :, chunk(who)] = mm3(split(kt[...]), split(outer)) - mm3(
            split(opv[:, 256:512]), split(lanes(x1, who))
        )
        return carry

    lax.fori_loop(0, 4, known, 0)
    k3[...] = -mm3(split(k3[...]), split(sinv[...]))
    gg3.wait()
    gx2.wait()

    def finish(who, carry):
        out[0, :, chunk(who)] += mm3(split(k3[...]), split(lanes(g3, who))) - mm3(
            split(kv2[...]), split(lanes(x2, who))
        )
        return carry

    lax.fori_loop(0, 4, finish, 0)
    for cond, make in sends:
        if cond is None:
            make().wait_send()
        else:
            pl.when(cond)(lambda make=make: make().wait_send())
    assert count[0] <= NSEM and local_count[0] <= 16


def on_device(leaf_maps, impedance, sources, top_trace, interior_op):
    anywhere = pl.BlockSpec(memory_space=pltpu.HBM)
    vm = lambda *shape: pltpu.VMEM(shape, F32)
    return pl.pallas_call(
        kernel,
        out_shape=jax.ShapeDtypeStruct((1, 256, 1024), F32),
        in_specs=[anywhere] * 5,
        out_specs=pl.BlockSpec(memory_space=pltpu.VMEM),
        scratch_shapes=[
            vm(2, 128, 128), vm(2, 128, 128), vm(2, 128, 128), vm(2, 2, 256, 128), vm(2, 256, 128),
            vm(2, 128, 128), vm(4, 2, 128, 256),
            vm(4, 2, 256, 128), vm(4, 2, 256, 128), vm(4, 2, 256, 128),
            vm(2, 1, 512), vm(2, 512, 128), vm(256, 128), vm(256, 512),
            vm(2, 3, 128, 128), vm(2, 2, 256, 128), vm(2, 2, 128, 128), vm(2, 384, 128),
            vm(2, 3, 128, 128), vm(2, 256, 128),
            vm(128, 128), vm(128, 128), vm(256, 256), vm(256, 640), vm(256, 512), vm(256, 256),
            vm(256, 256), vm(256, 256), vm(256, 256),
            pltpu.SemaphoreType.DMA((NSEM,)), pltpu.SemaphoreType.DMA((16,)),
        ],
        compiler_params=pltpu.CompilerParams(
            collective_id=0, has_side_effects=True, vmem_limit_bytes=63 * 2**20
        ),
        name="merge_solve",
    )(leaf_maps, impedance, sources, top_trace, interior_op)


def solution(mesh):
    return jax.shard_map(
        on_device,
        mesh=mesh,
        in_specs=(
            P("sub", None, "src"),
            P("sub", None),
            P("sub", None, "src"),
            P(None, None, "src"),
            P("sub", "src", None),
        ),
        out_specs=P("sub", "src", None),
        check_vma=False,
    )
```

```python
import jax
import jax.numpy as jnp
from jax import lax
from jax.experimental import pallas as pl
from jax.experimental.pallas import tpu as pltpu
from jax.sharding import PartitionSpec as P

F32 = jnp.float32
MESH = pl.DeviceIdType.MESH
NN = ((1,), (0,))
TN = ((0,), (0,))
NT = ((1,), (1,))
NSEM = 256


def mm(a, b, dims=NN):
    return lax.dot_general(
        a, b, (dims, ((), ())), precision=lax.Precision.HIGHEST, preferred_element_type=F32
    )


def split(a):
    high = a.astype(jnp.bfloat16)
    return high, (a - high.astype(F32)).astype(jnp.bfloat16)


def mm3(a, b, dims=NN):
    dot = lambda p, q: lax.dot_general(p, q, (dims, ((), ())), preferred_element_type=F32)
    return dot(a[0], b[0]) + (dot(a[0], b[1]) + dot(a[1], b[0]))


def tile_steps(panel, at, k):
    lane = lax.broadcasted_iota(jnp.int32, (8, 128), 1)
    row = lax.broadcasted_iota(jnp.int32, (8, 128), 0)
    column = lambda v, j: jnp.take_along_axis(v, jnp.full(v.shape, k + j, jnp.int32), axis=1)
    spread = lambda v, i: jnp.broadcast_to(v[i : i + 1, :], (8, 128))
    tile = panel[at]
    cols = [column(tile, j) for j in range(8)]
    others = {u: [column(panel[u], j) for j in range(8)] for u in range(len(panel)) if u != at}
    for q in range(0, 8, 2):
        a, b, d = spread(cols[q], q), spread(cols[q + 1], q), spread(cols[q + 1], q + 1)
        r = 1.0 / (a * d - b * b)
        i00, i01, i11 = d * r, -(b * r), a * r
        pivots = (row >= q) & (row < q + 2)
        m0 = jnp.where(pivots, jnp.where(row == q, -1.0, 0.0), cols[q])
        m1 = jnp.where(pivots, jnp.where(row == q + 1, -1.0, 0.0), cols[q + 1])

        def change(t0, t1):
            return m0 * (i00 * t0 + i01 * t1) + m1 * (i01 * t0 + i11 * t1)

        for j in range(q + 2, 8):
            cols[j] = jnp.where(pivots, 0.0, cols[j]) - change(spread(cols[j], q), spread(cols[j], q + 1))
        l0, l1 = lane == k + q, lane == k + q + 1
        t0 = jnp.where(l0, 1.0, jnp.where(l1, 0.0, spread(tile, q)))
        t1 = jnp.where(l1, 1.0, jnp.where(l0, 0.0, spread(tile, q + 1)))
        tile = jnp.where(pivots | l0 | l1, 0.0, tile) - change(t0, t1)
    rows = [spread(tile, j) for j in range(8)]
    done = (lane >= k) & (lane < k + 8)

    def follow(u):
        terms = [x * r for x, r in zip(others[u], rows)]
        while len(terms) > 1:
            terms = [terms[i] + terms[i + 1] for i in range(0, len(terms), 2)]
        return jnp.where(done, 0.0, panel[u]) - terms[0]

    return [tile if u == at else follow(u) for u in range(len(panel))]


PANEL = 64


def invert_panels(m, start, stop):
    n = m.shape[0]
    lane = lax.broadcasted_iota(jnp.int32, (n, n), 1)

    def body(t, carry):
        r0 = pl.multiple_of(t * PANEL, PANEL)
        whole = m[...]
        tiles = [pl.ds(pl.multiple_of(r0 + 8 * i, 8), 8) for i in range(PANEL // 8)]
        panel = [m[i, :] for i in tiles]
        for at in range(PANEL // 8):
            panel = tile_steps(panel, at, r0 + 8 * at)
        inside = (lane >= r0) & (lane < r0 + PANEL)
        rows = jnp.concatenate(panel * (n // PANEL), axis=0)
        m[...] = jnp.where(inside, 0.0, whole) - mm(jnp.where(inside, whole, 0.0), rows)
        for i, tile in zip(tiles, panel):
            m[i, :] = tile
        return carry

    lax.fori_loop(start, stop, body, 0)


def diag_of(row):
    n = row.shape[1]
    here = lax.broadcasted_iota(jnp.int32, (n, n), 0) == lax.broadcasted_iota(jnp.int32, (n, n), 1)
    return jnp.where(here, row, 0.0)


def kernel(
    leaf, imp, src, top, iop, out,
    s11, s12, s22, bq, e0, e1, tt, x1, x2, g3, impb, hb, town, opv,
    ss2, se2, ee2, h2, ss3, h3,
    m1, m2, sinv, bb, k1s, kv2, kt, k3, sem, lsem,
):
    s = lax.axis_index("sub")
    y = lax.axis_index("src")
    c = s % 2
    x = s // 2 % 4
    z = s // 8
    beta = x % 2
    gamma = x // 2
    sib = s + 1 - 2 * c
    part2 = z * 8 + (x + 1 - 2 * beta) * 2 + c
    part3 = z * 8 + (3 - x) * 2 + c

    barrier = pltpu.get_barrier_semaphore()
    greet = [(s, (y + d) % 4) for d in (1, 2, 3)] + [(sib, y), (part2, y), (part3, y)]
    for device in greet:
        pl.semaphore_signal(barrier, inc=1, device_id=device, device_id_type=MESH)

    count = [0]
    sends = []

    def take(n):
        base = count[0]
        count[0] += n
        return base

    def push(source, dest, recv, device, cond=None):
        sent = take(1)

        def make():
            return pltpu.make_async_remote_copy(
                source, dest, sem.at[sent], sem.at[recv], device_id=device, device_id_type=MESH
            )

        make().start()
        sends.append((cond, make))

    def arrived(ref, recv):
        pltpu.make_async_remote_copy(
            ref, ref, sem.at[0], sem.at[recv], device_id=(sib, y), device_id_type=MESH
        ).wait_recv()

    class Gather:
        def __init__(self, buf):
            self.buf = buf
            self.recv = take(8)

        def start(self):
            mine = self.buf.at[y, c]
            for d in (1, 3, 2):
                push(mine, mine, self.recv + y * 2 + c, (s, (y + d) % 4))
            push(mine, mine, self.recv + y * 2 + c, (sib, y))

        def relay(self, steps=(1, 3, 2)):
            for d in steps:
                who = (y + d) % 4
                slot = self.buf.at[who, c]
                arrived(slot, self.recv + who * 2 + c)
                push(slot, slot, self.recv + who * 2 + c, (sib, y))

        def wait(self, steps=(0, 1, 3, 2)):
            for d in steps:
                who = (y + d) % 4
                arrived(self.buf.at[who, 1 - c], self.recv + who * 2 + 1 - c)

    class Spread:
        def __init__(self, owner, source, buf):
            self.owner, self.source, self.buf = owner, source, buf
            self.recv = take(2)
            self.local = pltpu.make_async_copy(source, buf.at[c], lsem.at[take_local()])

        def start(self):
            mine = self.buf.at[c]

            @pl.when(y == self.owner)
            def _():
                self.local.start()
                for d in (1, 3, 2):
                    push(self.source, mine, self.recv, (s, (self.owner + d) % 4), True)
                push(self.source, mine, self.recv + 1, (sib, y), True)

            for i in range(len(sends) - 4, len(sends)):
                sends[i] = (y == self.owner, sends[i][1])

        def relay(self):
            mine = self.buf.at[c]

            @pl.when(y != self.owner)
            def _():
                arrived(mine, self.recv)
                push(mine, mine, self.recv + 1, (sib, y), True)

            sends[-1] = (y != self.owner, sends[-1][1])

        def wait(self):
            @pl.when(y == self.owner)
            def _():
                self.local.wait()

            arrived(self.buf.at[1 - c], self.recv + 1)

    class Pair:
        def __init__(self, device):
            self.device = device
            self.recv = take(1)

        def start(self, ref):
            push(ref, ref, self.recv, self.device)

        def wait(self, ref):
            arrived(ref, self.recv)

    locals_ = []
    local_count = [0]

    def take_local():
        local_count[0] += 1
        return local_count[0] - 1

    def fetch(source, dest):
        copy = pltpu.make_async_copy(source, dest, lsem.at[take_local()])
        copy.start()
        locals_.append(copy)

    own_lanes = pl.ds(pl.multiple_of(c * 128, 128), 128)
    rows = lambda lo, n: leaf.at[0, pl.ds(lo, n), :]
    b11, b12, b22 = Spread(2, rows(256, 128), s11), Spread(3, rows(256, 128), s12), Spread(3, rows(384, 128), s22)
    bb0, bb1 = Spread(0, rows(256, 256), bq.at[0]), Spread(1, rows(256, 256), bq.at[1])
    be0, be1 = Spread(0, rows(0, 256), e0), Spread(1, rows(128, 128), e1)
    gt, gx1, gx2, gg3 = Gather(tt), Gather(x1), Gather(x2), Gather(g3)
    pimp, phb = Pair((sib, y)), Pair((sib, y))
    fetch(imp, impb.at[c])

    pl.semaphore_wait(barrier, len(greet))
    for piece in (b11, b12, b22, bb0, bb1, be0, be1):
        piece.start()
    push(imp, impb.at[c], pimp.recv, (sib, y))
    push(src.at[0, :, pl.ds(pl.multiple_of((1 - c) * 128, 128), 128)], hb.at[c], phb.recv, (sib, y))
    fetch(src.at[0, :, own_lanes], hb.at[c])
    fetch(top.at[z, pl.ds(pl.multiple_of(c * 256 + gamma * 128, 128), 128), :], tt.at[y, c])
    for h in range(2):
        quarter = pl.ds(pl.multiple_of(h * 256 + gamma * 128, 128), 128)
        fetch(top.at[z, quarter, own_lanes], town.at[pl.ds(h * 128, 128), :])
    fetch(iop.at[0], opv)
    b11.relay()
    b11.wait()
    pimp.wait(impb.at[1 - c])
    for copy in locals_:
        copy.wait()

    def eliminate(first, off, last, mid1, mid2, mid3, mid4):
        m1[...] = first
        invert_panels(m1, 0, 1)
        mid1()
        invert_panels(m1, 1, 2)
        mid2()
        i11 = m1[...]
        side = off()
        w = mm(i11, side)
        m2[...] = last() - mm(side, w, TN)
        invert_panels(m2, 0, 1)
        mid3()
        invert_panels(m2, 1, 2)
        mid4()
        i22 = m2[...]
        i12 = -mm(w, i22)
        sinv[0:128, 0:128] = i11 - mm(i12, w, NT)
        sinv[0:128, 128:256] = i12
        sinv[128:256, 0:128] = i12.T
        sinv[128:256, 128:256] = i22

    def nothing():
        pass

    ir = lambda k, lo: impb[k, 0:1, lo : lo + 128]

    def mid1():
        b12.relay()
        b22.relay()

    def mid2():
        b12.wait()
        b22.wait()

    def mid3():
        bb0.relay()
        bb1.relay()

    def mid4():
        be0.relay()
        be1.relay()
        gt.start()

    eliminate(
        s11[0] + s11[1] + diag_of(ir(0, 256) + ir(1, 256)),
        lambda: s12[0] + s12[1],
        lambda: s22[0] + s22[1] + diag_of(ir(0, 384) + ir(1, 384)),
        mid1, mid2, mid3, mid4,
    )
    bb0.wait()
    bb1.wait()
    for i, (q, k) in enumerate(((1, 0), (1, 1), (0, 0), (0, 1))):
        bb[:, i * 128 : i * 128 + 128] = bq[q, k]
    inverse, bs = split(sinv[...]), split(bb[:, 0:256])
    xs = mm3(inverse, bs)
    be0.wait()
    be1.wait()
    zs = mm3(bs, split(xs), TN)
    ss2[beta, 0] = e1[0] + diag_of(ir(0, 128)) - zs[0:128, 0:128]
    ss2[beta, 1] = -zs[0:128, 128:256]
    ss2[beta, 2] = e1[1] + diag_of(ir(1, 128)) - zs[128:256, 128:256]
    p20, p2s, r2s = Pair((part2, y)), Pair((part2, y)), Pair((sib, y))
    pse2, pee2, ph2 = (Pair((part2, y)) for _ in range(3))
    rse2, ree2 = Pair((sib, y)), Pair((sib, y))
    p20.start(ss2.at[beta, 0])
    p2s.start(ss2.at[beta, 1 + c])
    phb.wait(hb.at[1 - c])
    bb[:, 512:640] = hb[0, 256:512, :] + hb[1, 256:512, :]
    xr = mm3(inverse, split(bb[:, 256:640]))
    xrs = split(xr)
    zr = mm3(bs, xrs, TN)
    se2[beta, 0, 0:128, :] = e0[0, 128:256, :] - zr[0:128, 0:128]
    se2[beta, 0, 128:256, :] = -zr[128:256, 0:128]
    se2[beta, 1, 0:128, :] = -zr[0:128, 128:256]
    se2[beta, 1, 128:256, :] = e0[1, 128:256, :] - zr[128:256, 128:256]
    pse2.start(se2.at[beta, c])
    z1 = mm3(split(bb[:, 384:512]), xrs, TN)
    ee2[beta, 0] = -z1[:, 0:128]
    ee2[beta, 1] = e0[1, 0:128, :] + diag_of(ir(1, 0)) - z1[:, 128:256]
    pee2.start(ee2.at[beta, c])
    h2[beta, 0:128, :] = hb[0, 128:256, :] - zr[0:128, 256:384]
    h2[beta, 128:256, :] = hb[1, 128:256, :] - zr[128:256, 256:384]
    h2[beta, 256:384, :] = hb[1, 0:128, :] - z1[:, 256:384]
    ph2.start(h2.at[beta])
    x1[y, c] = xr[:, 256:384]

    op_s = split(opv[:, 256:512])
    o0, o1 = opv[:, 0:128], opv[:, 128:256]
    pick = lambda v: jnp.concatenate([jnp.where(c == k, v, jnp.zeros_like(v)) for k in range(2)], axis=1)
    kv2[...] = pick(o1) - mm3(op_s, split(xs))
    k1s[...] = pick(o0) - mm3(op_s, split(xr[:, 0:256]))

    other = 1 - beta

    def mid1():
        p2s.wait(ss2.at[other, 1 + c])
        r2s.start(ss2.at[other, 1 + c])
        gt.relay()
        gx1.start()

    def mid2():
        r2s.wait(ss2.at[other, 2 - c])

    def mid3():
        pse2.wait(se2.at[other, c])
        rse2.start(se2.at[other, c])

    def mid4():
        pee2.wait(ee2.at[other, c])
        ree2.start(ee2.at[other, c])

    p20.wait(ss2.at[other, 0])
    eliminate(
        ss2[0, 0] + ss2[1, 0], lambda: ss2[0, 1] + ss2[1, 1], lambda: ss2[0, 2] + ss2[1, 2],
        mid1, mid2, mid3, mid4,
    )
    rse2.wait(se2.at[other, 1 - c])
    for i, (k, q) in enumerate(((0, 1), (1, 1), (0, 0), (1, 0))):
        bb[:, i * 128 : i * 128 + 128] = se2[k, q]
    inverse, bs = split(sinv[...]), split(bb[:, 0:256])
    xs = mm3(inverse, bs)
    ree2.wait(ee2.at[other, 1 - c])
    zs = mm3(bs, split(xs), TN)
    ss3[gamma, 0] = ee2[0, 1] - zs[0:128, 0:128]
    ss3[gamma, 1] = -zs[0:128, 128:256]
    ss3[gamma, 2] = ee2[1, 1] - zs[128:256, 128:256]
    p30, p3s, r3s, ph3 = Pair((part3, y)), Pair((part3, y)), Pair((sib, y)), Pair((part3, y))
    p30.start(ss3.at[gamma, 0])
    p3s.start(ss3.at[gamma, 1 + c])
    ph2.wait(h2.at[other])
    bb[:, 512:640] = h2[0, 0:256, :] + h2[1, 0:256, :]
    xr = mm3(inverse, split(bb[:, 256:640]))
    zr = mm3(bs, split(xr), TN)
    h3[gamma, 0:128, :] = h2[0, 256:384, :] - zr[0:128, 256:384]
    h3[gamma, 128:256, :] = h2[1, 256:384, :] - zr[128:256, 256:384]
    bb[:, 0:256] = -zr[:, 0:256]
    bb[0:128, 0:128] += ee2[0, 0]
    bb[128:256, 128:256] += ee2[1, 0]
    h3[gamma] += mm3(split(bb[:, 0:256]), split(town[...]))
    ph3.start(h3.at[gamma])
    x2[y, c] = xr[:, 256:384]
    gx2.start()

    kvs = split(kv2[...])
    ko, ki = k1s[:, 0:128], k1s[:, 128:256]
    pick = lambda v: jnp.concatenate([jnp.where(beta == k, v, jnp.zeros_like(v)) for k in range(2)], axis=1)
    kt[...] = pick(ko) - mm3(kvs, split(xr[:, 0:256]))
    k3[...] = pick(ki) - mm3(kvs, split(xs))
    chunk = lambda who: pl.ds(pl.multiple_of(who * 256, 256), 256)
    lanes = lambda buf, who: jnp.concatenate([buf[who, 0], buf[who, 1]], axis=1)

    across = 1 - gamma

    def mid1():
        p3s.wait(ss3.at[across, 1 + c])
        r3s.start(ss3.at[across, 1 + c])
        ph3.wait(h3.at[across])
        g3[y, c] = h3[0] + h3[1]
        gg3.start()

    def mid2():
        gx1.relay()
        r3s.wait(ss3.at[across, 2 - c])

    def mid3():
        gx2.relay()

    p30.wait(ss3.at[across, 0])
    eliminate(
        ss3[0, 0] + ss3[1, 0], lambda: ss3[0, 1] + ss3[1, 1], lambda: ss3[0, 2] + ss3[1, 2],
        mid1, mid2, mid3, lambda: gg3.relay((1, 3)),
    )
    gt.wait()
    gx1.wait()

    def known(who, carry):
        outer = jnp.concatenate([tt[who, 0], tt[who, 1]], axis=0)
        out[0, :, chunk(who)] = mm3(split(kt[...]), split(outer)) - mm3(
            split(opv[:, 256:512]), split(lanes(x1, who))
        )
        return carry

    lax.fori_loop(0, 4, known, 0)
    k3[...] = -mm3(split(k3[...]), split(sinv[...]))
    gx2.wait()
    left = split(jnp.concatenate([k3[...], kv2[...]], axis=1))
    for d in (0, 1, 3, 2):
        who = (y + d) % 4
        if d == 2:
            gg3.relay((2,))
        gg3.wait((d,))
        right = jnp.concatenate([lanes(g3, who), -lanes(x2, who)], axis=0)
        out[0, :, chunk(who)] += mm3(left, split(right))
    for cond, make in sends:
        if cond is None:
            make().wait_send()
        else:
            pl.when(cond)(lambda make=make: make().wait_send())
    assert count[0] <= NSEM and local_count[0] <= 16


def on_device(leaf_maps, impedance, sources, top_trace, interior_op):
    anywhere = pl.BlockSpec(memory_space=pltpu.HBM)
    vm = lambda *shape: pltpu.VMEM(shape, F32)
    return pl.pallas_call(
        kernel,
        out_shape=jax.ShapeDtypeStruct((1, 256, 1024), F32),
        in_specs=[anywhere] * 5,
        out_specs=pl.BlockSpec(memory_space=pltpu.VMEM),
        scratch_shapes=[
            vm(2, 128, 128), vm(2, 128, 128), vm(2, 128, 128), vm(2, 2, 256, 128), vm(2, 256, 128),
            vm(2, 128, 128), vm(4, 2, 128, 256),
            vm(4, 2, 256, 128), vm(4, 2, 256, 128), vm(4, 2, 256, 128),
            vm(2, 1, 512), vm(2, 512, 128), vm(256, 128), vm(256, 512),
            vm(2, 3, 128, 128), vm(2, 2, 256, 128), vm(2, 2, 128, 128), vm(2, 384, 128),
            vm(2, 3, 128, 128), vm(2, 256, 128),
            vm(128, 128), vm(128, 128), vm(256, 256), vm(256, 640), vm(256, 256),
            vm(256, 256), vm(256, 256), vm(256, 256),
            pltpu.SemaphoreType.DMA((NSEM,)), pltpu.SemaphoreType.DMA((16,)),
        ],
        compiler_params=pltpu.CompilerParams(
            collective_id=0, has_side_effects=True, vmem_limit_bytes=63 * 2**20
        ),
        name="merge_solve",
    )(leaf_maps, impedance, sources, top_trace, interior_op)


def solution(mesh):
    return jax.shard_map(
        on_device,
        mesh=mesh,
        in_specs=(
            P("sub", None, "src"),
            P("sub", None),
            P("sub", None, "src"),
            P(None, None, "src"),
            P("sub", "src", None),
        ),
        out_specs=P("sub", "src", None),
        check_vma=False,
    )
```

```python
import jax
import jax.numpy as jnp
from jax import lax
from jax.experimental import pallas as pl
from jax.experimental.pallas import tpu as pltpu
from jax.sharding import PartitionSpec as P

F32 = jnp.float32
MESH = pl.DeviceIdType.MESH
NN = ((1,), (0,))
TN = ((0,), (0,))
NT = ((1,), (1,))
NSEM = 256


def mm(a, b, dims=NN):
    return lax.dot_general(
        a, b, (dims, ((), ())), precision=lax.Precision.HIGHEST, preferred_element_type=F32
    )


def split(a):
    high = a.astype(jnp.bfloat16)
    return high, (a - high.astype(F32)).astype(jnp.bfloat16)


def mm3(a, b, dims=NN):
    dot = lambda p, q: lax.dot_general(p, q, (dims, ((), ())), preferred_element_type=F32)
    return dot(a[0], b[0]) + (dot(a[0], b[1]) + dot(a[1], b[0]))


def tile_steps(panel, at, k):
    lane = lax.broadcasted_iota(jnp.int32, (8, 128), 1)
    row = lax.broadcasted_iota(jnp.int32, (8, 128), 0)
    column = lambda v, j: jnp.take_along_axis(v, jnp.full(v.shape, k + j, jnp.int32), axis=1)
    spread = lambda v, i: jnp.broadcast_to(v[i : i + 1, :], (8, 128))
    tile = panel[at]
    cols = [column(tile, j) for j in range(8)]
    others = {u: [column(panel[u], j) for j in range(8)] for u in range(len(panel)) if u != at}
    for q in range(0, 8, 2):
        a, b, d = spread(cols[q], q), spread(cols[q + 1], q), spread(cols[q + 1], q + 1)
        r = 1.0 / (a * d - b * b)
        i00, i01, i11 = d * r, -(b * r), a * r
        pivots = (row >= q) & (row < q + 2)
        m0 = jnp.where(pivots, jnp.where(row == q, -1.0, 0.0), cols[q])
        m1 = jnp.where(pivots, jnp.where(row == q + 1, -1.0, 0.0), cols[q + 1])

        def change(t0, t1):
            return m0 * (i00 * t0 + i01 * t1) + m1 * (i01 * t0 + i11 * t1)

        for j in range(q + 2, 8):
            cols[j] = jnp.where(pivots, 0.0, cols[j]) - change(spread(cols[j], q), spread(cols[j], q + 1))
        l0, l1 = lane == k + q, lane == k + q + 1
        t0 = jnp.where(l0, 1.0, jnp.where(l1, 0.0, spread(tile, q)))
        t1 = jnp.where(l1, 1.0, jnp.where(l0, 0.0, spread(tile, q + 1)))
        tile = jnp.where(pivots | l0 | l1, 0.0, tile) - change(t0, t1)
    rows = [spread(tile, j) for j in range(8)]
    done = (lane >= k) & (lane < k + 8)

    def follow(u):
        terms = [x * r for x, r in zip(others[u], rows)]
        while len(terms) > 1:
            terms = [terms[i] + terms[i + 1] for i in range(0, len(terms), 2)]
        return jnp.where(done, 0.0, panel[u]) - terms[0]

    return [tile if u == at else follow(u) for u in range(len(panel))]


PANEL = 64


def invert_panel(m, r0):
    n = m.shape[0]
    lane = lax.broadcasted_iota(jnp.int32, (n, n), 1)
    r0 = pl.multiple_of(r0, PANEL)
    whole = m[...]
    tiles = [pl.ds(pl.multiple_of(r0 + 8 * i, 8), 8) for i in range(PANEL // 8)]
    panel = [m[i, :] for i in tiles]
    for at in range(PANEL // 8):
        panel = tile_steps(panel, at, r0 + 8 * at)
    inside = (lane >= r0) & (lane < r0 + PANEL)
    rows = jnp.concatenate(panel * (n // PANEL), axis=0)
    m[...] = jnp.where(inside, 0.0, whole) - mm(jnp.where(inside, whole, 0.0), rows)
    for i, tile in zip(tiles, panel):
        m[i, :] = tile


def diag_of(row):
    n = row.shape[1]
    here = lax.broadcasted_iota(jnp.int32, (n, n), 0) == lax.broadcasted_iota(jnp.int32, (n, n), 1)
    return jnp.where(here, row, 0.0)


def kernel(
    leaf, imp, src, top, iop, out,
    s11, s12, s22, bq, e0, e1, tt, x1, x2, g3, impb, hb, town, opv,
    ss2, se2, ee2, h2, ss3, h3,
    mb, ws, sinv, bb, k1s, kv2, kt, k3, sem, lsem,
):
    s = lax.axis_index("sub")
    y = lax.axis_index("src")
    c = s % 2
    x = s // 2 % 4
    z = s // 8
    beta = x % 2
    gamma = x // 2
    sib = s + 1 - 2 * c
    part2 = z * 8 + (x + 1 - 2 * beta) * 2 + c
    part3 = z * 8 + (3 - x) * 2 + c

    barrier = pltpu.get_barrier_semaphore()
    greet = [(s, (y + d) % 4) for d in (1, 2, 3)] + [(sib, y), (part2, y), (part3, y)]
    for device in greet:
        pl.semaphore_signal(barrier, inc=1, device_id=device, device_id_type=MESH)

    count = [0]
    sends = []

    def take(n):
        base = count[0]
        count[0] += n
        return base

    def push(get, cond=None):
        sent = take(1)

        def make():
            source, dest, recv, device = get()
            return pltpu.make_async_remote_copy(
                source, dest, sem.at[sent], sem.at[recv], device_id=device, device_id_type=MESH
            )

        make().start()
        sends.append((cond, make))

    def arrived(ref, recv):
        pltpu.make_async_remote_copy(
            ref, ref, sem.at[0], sem.at[recv], device_id=(sib, y), device_id_type=MESH
        ).wait_recv()

    class Gather:
        def __init__(self, buf):
            self.buf = buf
            self.recv = take(8)

        def start(self):
            def to(device):
                mine = self.buf.at[y, c]
                return mine, mine, self.recv + y * 2 + c, device

            for d in (1, 3, 2):
                push(lambda d=d: to((s, (y + d) % 4)))
            push(lambda: to((sib, y)))

        def relay(self, steps=(1, 3, 2)):
            def onward(d):
                who = (y + d) % 4
                slot = self.buf.at[who, c]
                return slot, slot, self.recv + who * 2 + c, (sib, y)

            for d in steps:
                slot, _, recv, _ = onward(d)
                arrived(slot, recv)
                push(lambda d=d: onward(d))

        def wait(self, steps=(0, 1, 3, 2)):
            for d in steps:
                who = (y + d) % 4
                arrived(self.buf.at[who, 1 - c], self.recv + who * 2 + 1 - c)

    class Spread:
        def __init__(self, owner, source, buf):
            self.owner, self.source, self.buf = owner, source, buf
            self.recv = take(2)
            self.local = pltpu.make_async_copy(source, buf.at[c], lsem.at[take_local()])

        def start(self):
            owns = lambda: y == self.owner

            @pl.when(owns())
            def _():
                self.local.start()
                for d in (1, 3, 2):
                    there = (self.owner + d) % 4
                    push(lambda there=there: (self.source, self.buf.at[c], self.recv, (s, there)), owns)
                push(lambda: (self.source, self.buf.at[c], self.recv + 1, (sib, y)), owns)

        def relay(self):
            lacks = lambda: y != self.owner

            @pl.when(lacks())
            def _():
                arrived(self.buf.at[c], self.recv)
                push(lambda: (self.buf.at[c], self.buf.at[c], self.recv + 1, (sib, y)), lacks)

        def wait(self):
            @pl.when(y == self.owner)
            def _():
                self.local.wait()

            arrived(self.buf.at[1 - c], self.recv + 1)

    class Pair:
        def __init__(self, device):
            self.device = device
            self.recv = take(1)

        def start(self, ref):
            push(lambda: (ref(), ref(), self.recv, self.device))

        def wait(self, ref):
            arrived(ref, self.recv)

    locals_ = []
    local_count = [0]

    def take_local():
        local_count[0] += 1
        return local_count[0] - 1

    def fetch(source, dest):
        copy = pltpu.make_async_copy(source, dest, lsem.at[take_local()])
        copy.start()
        locals_.append(copy)

    own_lanes = pl.ds(pl.multiple_of(c * 128, 128), 128)
    rows = lambda lo, n: leaf.at[0, pl.ds(lo, n), :]
    b11, b12, b22 = Spread(2, rows(256, 128), s11), Spread(3, rows(256, 128), s12), Spread(3, rows(384, 128), s22)
    bb0, bb1 = Spread(0, rows(256, 256), bq.at[0]), Spread(1, rows(256, 256), bq.at[1])
    be0, be1 = Spread(0, rows(0, 256), e0), Spread(1, rows(128, 128), e1)
    gt, gx1, gx2, gg3 = Gather(tt), Gather(x1), Gather(x2), Gather(g3)
    pimp, phb = Pair((sib, y)), Pair((sib, y))
    fetch(imp, impb.at[c])

    pl.semaphore_wait(barrier, len(greet))
    for piece in (b11, b12, b22, bb0, bb1, be0, be1):
        piece.start()
    push(lambda: (imp, impb.at[c], pimp.recv, (sib, y)))
    push(
        lambda: (src.at[0, :, pl.ds(pl.multiple_of((1 - c) * 128, 128), 128)], hb.at[c], phb.recv, (sib, y))
    )
    fetch(src.at[0, :, own_lanes], hb.at[c])
    fetch(top.at[z, pl.ds(pl.multiple_of(c * 256 + gamma * 128, 128), 128), :], tt.at[y, c])
    for h in range(2):
        quarter = pl.ds(pl.multiple_of(h * 256 + gamma * 128, 128), 128)
        fetch(top.at[z, quarter, own_lanes], town.at[pl.ds(h * 128, 128), :])
    fetch(iop.at[0], opv)
    b11.relay()
    b11.wait()
    pimp.wait(impb.at[1 - c])
    for copy in locals_:
        copy.wait()

    hooks = []

    def eliminate(off, last, mid1, mid2, mid3, then):
        def middle():
            mid2()
            side = off()
            w = mm(mb[0], side)
            ws[...] = w
            mb[1] = last() - mm(side, w, TN)

        def end():
            i12 = -mm(ws[...], mb[1])
            sinv[0:128, 0:128] = mb[0] - mm(i12, ws[...], NT)
            sinv[0:128, 128:256] = i12
            sinv[128:256, 0:128] = i12.T
            sinv[128:256, 128:256] = mb[1]
            then()

        hooks.extend([mid1, middle, mid3, end])

    p20, p2s, r2s = Pair((part2, y)), Pair((part2, y)), Pair((sib, y))
    pse2, pee2, ph2 = (Pair((part2, y)) for _ in range(3))
    rse2, ree2 = Pair((sib, y)), Pair((sib, y))
    p30, p3s, r3s, ph3 = Pair((part3, y)), Pair((part3, y)), Pair((sib, y)), Pair((part3, y))
    other = 1 - beta
    across = 1 - gamma
    chunk = lambda who: pl.ds(pl.multiple_of(who * 256, 256), 256)
    lanes = lambda buf, who: jnp.concatenate([buf[who, 0], buf[who, 1]], axis=1)

    ir = lambda k, lo: impb[k, 0:1, lo : lo + 128]

    def mid1():
        b12.relay()
        b22.relay()

    def mid2():
        b12.wait()
        b22.wait()

    def mid3():
        bb0.relay()
        bb1.relay()

    def mid4():
        be0.relay()
        be1.relay()
        gt.start()

    def after1():
        mid4()
        bb0.wait()
        bb1.wait()
        for i, (q, k) in enumerate(((1, 0), (1, 1), (0, 0), (0, 1))):
            bb[:, i * 128 : i * 128 + 128] = bq[q, k]
        inverse, bs = split(sinv[...]), split(bb[:, 0:256])
        xs = mm3(inverse, bs)
        be0.wait()
        be1.wait()
        zs = mm3(bs, split(xs), TN)
        ss2[beta, 0] = e1[0] + diag_of(ir(0, 128)) - zs[0:128, 0:128]
        ss2[beta, 1] = -zs[0:128, 128:256]
        ss2[beta, 2] = e1[1] + diag_of(ir(1, 128)) - zs[128:256, 128:256]
        p20.start(lambda: ss2.at[beta, 0])
        p2s.start(lambda: ss2.at[beta, 1 + c])
        phb.wait(hb.at[1 - c])
        bb[:, 512:640] = hb[0, 256:512, :] + hb[1, 256:512, :]
        xr = mm3(inverse, split(bb[:, 256:640]))
        xrs = split(xr)
        zr = mm3(bs, xrs, TN)
        se2[beta, 0, 0:128, :] = e0[0, 128:256, :] - zr[0:128, 0:128]
        se2[beta, 0, 128:256, :] = -zr[128:256, 0:128]
        se2[beta, 1, 0:128, :] = -zr[0:128, 128:256]
        se2[beta, 1, 128:256, :] = e0[1, 128:256, :] - zr[128:256, 128:256]
        pse2.start(lambda: se2.at[beta, c])
        z1 = mm3(split(bb[:, 384:512]), xrs, TN)
        ee2[beta, 0] = -z1[:, 0:128]
        ee2[beta, 1] = e0[1, 0:128, :] + diag_of(ir(1, 0)) - z1[:, 128:256]
        pee2.start(lambda: ee2.at[beta, c])
        h2[beta, 0:128, :] = hb[0, 128:256, :] - zr[0:128, 256:384]
        h2[beta, 128:256, :] = hb[1, 128:256, :] - zr[128:256, 256:384]
        h2[beta, 256:384, :] = hb[1, 0:128, :] - z1[:, 256:384]
        ph2.start(lambda: h2.at[beta])
        x1[y, c] = xr[:, 256:384]

        op_s = split(opv[:, 256:512])
        o0, o1 = opv[:, 0:128], opv[:, 128:256]
        pick = lambda v: jnp.concatenate([jnp.where(c == k, v, jnp.zeros_like(v)) for k in range(2)], axis=1)
        kv2[...] = pick(o1) - mm3(op_s, split(xs))
        k1s[...] = pick(o0) - mm3(op_s, split(xr[:, 0:256]))
        p20.wait(ss2.at[other, 0])
        mb[0] = ss2[0, 0] + ss2[1, 0]

    mb[0] = s11[0] + s11[1] + diag_of(ir(0, 256) + ir(1, 256))
    eliminate(
        lambda: s12[0] + s12[1],
        lambda: s22[0] + s22[1] + diag_of(ir(0, 384) + ir(1, 384)),
        mid1, mid2, mid3, after1,
    )


    def mid1():
        p2s.wait(ss2.at[other, 1 + c])
        r2s.start(lambda: ss2.at[other, 1 + c])
        gt.relay()
        gx1.start()

    def mid2():
        r2s.wait(ss2.at[other, 2 - c])

    def mid3():
        pse2.wait(se2.at[other, c])
        rse2.start(lambda: se2.at[other, c])

    def after2():
        pee2.wait(ee2.at[other, c])
        ree2.start(lambda: ee2.at[other, c])
        rse2.wait(se2.at[other, 1 - c])
        for i, (k, q) in enumerate(((0, 1), (1, 1), (0, 0), (1, 0))):
            bb[:, i * 128 : i * 128 + 128] = se2[k, q]
        inverse, bs = split(sinv[...]), split(bb[:, 0:256])
        xs = mm3(inverse, bs)
        ree2.wait(ee2.at[other, 1 - c])
        zs = mm3(bs, split(xs), TN)
        ss3[gamma, 0] = ee2[0, 1] - zs[0:128, 0:128]
        ss3[gamma, 1] = -zs[0:128, 128:256]
        ss3[gamma, 2] = ee2[1, 1] - zs[128:256, 128:256]
        p30.start(lambda: ss3.at[gamma, 0])
        p3s.start(lambda: ss3.at[gamma, 1 + c])
        ph2.wait(h2.at[other])
        bb[:, 512:640] = h2[0, 0:256, :] + h2[1, 0:256, :]
        xr = mm3(inverse, split(bb[:, 256:640]))
        zr = mm3(bs, split(xr), TN)
        h3[gamma, 0:128, :] = h2[0, 256:384, :] - zr[0:128, 256:384]
        h3[gamma, 128:256, :] = h2[1, 256:384, :] - zr[128:256, 256:384]
        bb[:, 0:256] = -zr[:, 0:256]
        bb[0:128, 0:128] += ee2[0, 0]
        bb[128:256, 128:256] += ee2[1, 0]
        h3[gamma] += mm3(split(bb[:, 0:256]), split(town[...]))
        ph3.start(lambda: h3.at[gamma])
        x2[y, c] = xr[:, 256:384]
        gx2.start()

        kvs = split(kv2[...])
        ko, ki = k1s[:, 0:128], k1s[:, 128:256]
        pick = lambda v: jnp.concatenate([jnp.where(beta == k, v, jnp.zeros_like(v)) for k in range(2)], axis=1)
        kt[...] = pick(ko) - mm3(kvs, split(xr[:, 0:256]))
        k3[...] = pick(ki) - mm3(kvs, split(xs))
        p30.wait(ss3.at[across, 0])
        mb[0] = ss3[0, 0] + ss3[1, 0]

    eliminate(
        lambda: ss2[0, 1] + ss2[1, 1], lambda: ss2[0, 2] + ss2[1, 2], mid1, mid2, mid3, after2
    )


    def mid1():
        p3s.wait(ss3.at[across, 1 + c])
        r3s.start(lambda: ss3.at[across, 1 + c])
        ph3.wait(h3.at[across])
        g3[y, c] = h3[0] + h3[1]
        gg3.start()

    def mid2():
        gx1.relay()
        r3s.wait(ss3.at[across, 2 - c])

    def mid3():
        gx2.relay()

    eliminate(
        lambda: ss3[0, 1] + ss3[1, 1], lambda: ss3[0, 2] + ss3[1, 2],
        mid1, mid2, mid3, lambda: gg3.relay((1, 3)),
    )

    def step(at, carry):
        invert_panel(mb.at[at // 2 % 2], at % 2 * PANEL)
        for k, hook in enumerate(hooks):
            pl.when(at == k)(hook)
        return carry

    lax.fori_loop(0, len(hooks), step, 0)
    gt.wait()
    gx1.wait()

    def known(who, carry):
        outer = jnp.concatenate([tt[who, 0], tt[who, 1]], axis=0)
        out[0, :, chunk(who)] = mm3(split(kt[...]), split(outer)) - mm3(
            split(opv[:, 256:512]), split(lanes(x1, who))
        )
        return carry

    lax.fori_loop(0, 4, known, 0)
    k3[...] = -mm3(split(k3[...]), split(sinv[...]))
    gx2.wait()
    left = split(jnp.concatenate([k3[...], kv2[...]], axis=1))
    for d in (0, 1, 3, 2):
        who = (y + d) % 4
        if d == 2:
            gg3.relay((2,))
        gg3.wait((d,))
        right = jnp.concatenate([lanes(g3, who), -lanes(x2, who)], axis=0)
        out[0, :, chunk(who)] += mm3(left, split(right))
    for cond, make in sends:
        if cond is None:
            make().wait_send()
        else:
            pl.when(cond())(lambda make=make: make().wait_send())
    assert count[0] <= NSEM and local_count[0] <= 16


def on_device(leaf_maps, impedance, sources, top_trace, interior_op):
    anywhere = pl.BlockSpec(memory_space=pltpu.HBM)
    vm = lambda *shape: pltpu.VMEM(shape, F32)
    return pl.pallas_call(
        kernel,
        out_shape=jax.ShapeDtypeStruct((1, 256, 1024), F32),
        in_specs=[anywhere] * 5,
        out_specs=pl.BlockSpec(memory_space=pltpu.VMEM),
        scratch_shapes=[
            vm(2, 128, 128), vm(2, 128, 128), vm(2, 128, 128), vm(2, 2, 256, 128), vm(2, 256, 128),
            vm(2, 128, 128), vm(4, 2, 128, 256),
            vm(4, 2, 256, 128), vm(4, 2, 256, 128), vm(4, 2, 256, 128),
            vm(2, 1, 512), vm(2, 512, 128), vm(256, 128), vm(256, 512),
            vm(2, 3, 128, 128), vm(2, 2, 256, 128), vm(2, 2, 128, 128), vm(2, 384, 128),
            vm(2, 3, 128, 128), vm(2, 256, 128),
            vm(2, 128, 128), vm(128, 128), vm(256, 256), vm(256, 640), vm(256, 256),
            vm(256, 256), vm(256, 256), vm(256, 256),
            pltpu.SemaphoreType.DMA((NSEM,)), pltpu.SemaphoreType.DMA((16,)),
        ],
        compiler_params=pltpu.CompilerParams(
            collective_id=0, has_side_effects=True, vmem_limit_bytes=40 * 2**20
        ),
        name="merge_solve",
    )(*[pltpu.with_memory_space_constraint(a, pltpu.HBM) for a in (leaf_maps, impedance, sources, top_trace, interior_op)])


def solution(mesh):
    return jax.shard_map(
        on_device,
        mesh=mesh,
        in_specs=(
            P("sub", None, "src"),
            P("sub", None),
            P("sub", None, "src"),
            P(None, None, "src"),
            P("sub", "src", None),
        ),
        out_specs=P("sub", "src", None),
        check_vma=False,
    )
```

```python
import jax
import jax.numpy as jnp
from jax import lax
from jax.experimental import pallas as pl
from jax.experimental.pallas import tpu as pltpu
from jax.sharding import PartitionSpec as P

F32 = jnp.float32
MESH = pl.DeviceIdType.MESH
NN = ((1,), (0,))
TN = ((0,), (0,))
NT = ((1,), (1,))
NSEM = 256


def mm(a, b, dims=NN):
    return lax.dot_general(
        a, b, (dims, ((), ())), precision=lax.Precision.HIGHEST, preferred_element_type=F32
    )


def split(a):
    high = a.astype(jnp.bfloat16)
    return high, (a - high.astype(F32)).astype(jnp.bfloat16)


def mm3(a, b, dims=NN):
    dot = lambda p, q: lax.dot_general(p, q, (dims, ((), ())), preferred_element_type=F32)
    return dot(a[0], b[0]) + (dot(a[0], b[1]) + dot(a[1], b[0]))


def tile_steps(panel, at, k):
    lane = lax.broadcasted_iota(jnp.int32, (8, 128), 1)
    row = lax.broadcasted_iota(jnp.int32, (8, 128), 0)
    column = lambda v, j: jnp.take_along_axis(v, jnp.full(v.shape, k + j, jnp.int32), axis=1)
    spread = lambda v, i: jnp.broadcast_to(v[i : i + 1, :], (8, 128))
    tile = panel[at]
    cols = [column(tile, j) for j in range(8)]
    others = {u: [column(panel[u], j) for j in range(8)] for u in range(len(panel)) if u != at}
    for q in range(0, 8, 2):
        a, b, d = spread(cols[q], q), spread(cols[q + 1], q), spread(cols[q + 1], q + 1)
        r = 1.0 / (a * d - b * b)
        i00, i01, i11 = d * r, -(b * r), a * r
        pivots = (row >= q) & (row < q + 2)
        m0 = jnp.where(pivots, jnp.where(row == q, -1.0, 0.0), cols[q])
        m1 = jnp.where(pivots, jnp.where(row == q + 1, -1.0, 0.0), cols[q + 1])

        def change(t0, t1):
            return m0 * (i00 * t0 + i01 * t1) + m1 * (i01 * t0 + i11 * t1)

        for j in range(q + 2, 8):
            cols[j] = jnp.where(pivots, 0.0, cols[j]) - change(spread(cols[j], q), spread(cols[j], q + 1))
        l0, l1 = lane == k + q, lane == k + q + 1
        t0 = jnp.where(l0, 1.0, jnp.where(l1, 0.0, spread(tile, q)))
        t1 = jnp.where(l1, 1.0, jnp.where(l0, 0.0, spread(tile, q + 1)))
        tile = jnp.where(pivots | l0 | l1, 0.0, tile) - change(t0, t1)
    rows = [spread(tile, j) for j in range(8)]
    done = (lane >= k) & (lane < k + 8)

    def follow(u):
        terms = [x * r for x, r in zip(others[u], rows)]
        while len(terms) > 1:
            terms = [terms[i] + terms[i + 1] for i in range(0, len(terms), 2)]
        return jnp.where(done, 0.0, panel[u]) - terms[0]

    return [tile if u == at else follow(u) for u in range(len(panel))]


PANEL = 64


def invert_panel(m, r0):
    n = m.shape[0]
    lane = lax.broadcasted_iota(jnp.int32, (n, n), 1)
    r0 = pl.multiple_of(r0, PANEL)
    whole = m[...]
    tiles = [pl.ds(pl.multiple_of(r0 + 8 * i, 8), 8) for i in range(PANEL // 8)]
    panel = [m[i, :] for i in tiles]
    for at in range(PANEL // 8):
        panel = tile_steps(panel, at, r0 + 8 * at)
    inside = (lane >= r0) & (lane < r0 + PANEL)
    rows = jnp.concatenate(panel * (n // PANEL), axis=0)
    m[...] = jnp.where(inside, 0.0, whole) - mm(jnp.where(inside, whole, 0.0), rows)
    for i, tile in zip(tiles, panel):
        m[i, :] = tile


def diag_of(row):
    n = row.shape[1]
    here = lax.broadcasted_iota(jnp.int32, (n, n), 0) == lax.broadcasted_iota(jnp.int32, (n, n), 1)
    return jnp.where(here, row, 0.0)


def kernel(
    leaf, imp, src, top, iop, out,
    s11, s12, s22, bq, e0, e1, tt, x1, x2, g3, impb, hb, town, opv,
    ss2, se2, ee2, h2, ss3, h3,
    mb, ws, sinv, bb, k1s, kv2, k3, sem, lsem,
):
    s = lax.axis_index("sub")
    y = lax.axis_index("src")
    c = s % 2
    x = s // 2 % 4
    z = s // 8
    beta = x % 2
    gamma = x // 2
    sib = s + 1 - 2 * c
    part2 = z * 8 + (x + 1 - 2 * beta) * 2 + c
    part3 = z * 8 + (3 - x) * 2 + c

    barrier = pltpu.get_barrier_semaphore()
    greet = [(s, (y + d) % 4) for d in (1, 2, 3)] + [(sib, y), (part2, y), (part3, y)]
    for device in greet:
        pl.semaphore_signal(barrier, inc=1, device_id=device, device_id_type=MESH)

    count = [0]
    sends = []

    def take(n):
        base = count[0]
        count[0] += n
        return base

    def push(get, cond=None):
        sent = take(1)

        def make():
            source, dest, recv, device = get()
            return pltpu.make_async_remote_copy(
                source, dest, sem.at[sent], sem.at[recv], device_id=device, device_id_type=MESH
            )

        make().start()
        sends.append((cond, make))

    def arrived(ref, recv):
        pltpu.make_async_remote_copy(
            ref, ref, sem.at[0], sem.at[recv], device_id=(sib, y), device_id_type=MESH
        ).wait_recv()

    class Gather:
        def __init__(self, buf):
            self.buf = buf
            self.recv = take(8)

        def start(self):
            def to(device):
                mine = self.buf.at[y, c]
                return mine, mine, self.recv + y * 2 + c, device

            for d in (1, 3, 2):
                push(lambda d=d: to((s, (y + d) % 4)))
            push(lambda: to((sib, y)))

        def relay(self, steps=(1, 3, 2)):
            def onward(d):
                who = (y + d) % 4
                slot = self.buf.at[who, c]
                return slot, slot, self.recv + who * 2 + c, (sib, y)

            for d in steps:
                slot, _, recv, _ = onward(d)
                arrived(slot, recv)
                push(lambda d=d: onward(d))

        def wait(self, steps=(0, 1, 3, 2)):
            for d in steps:
                who = (y + d) % 4
                arrived(self.buf.at[who, 1 - c], self.recv + who * 2 + 1 - c)

    class Spread:
        def __init__(self, owner, source, buf):
            self.owner, self.source, self.buf = owner, source, buf
            self.recv = take(2)
            self.local = pltpu.make_async_copy(source, buf.at[c], lsem.at[take_local()])

        def start(self):
            owns = lambda: y == self.owner

            @pl.when(owns())
            def _():
                self.local.start()
                for d in (1, 3, 2):
                    there = (self.owner + d) % 4
                    push(lambda there=there: (self.source, self.buf.at[c], self.recv, (s, there)), owns)
                push(lambda: (self.source, self.buf.at[c], self.recv + 1, (sib, y)), owns)

        def relay(self):
            lacks = lambda: y != self.owner

            @pl.when(lacks())
            def _():
                arrived(self.buf.at[c], self.recv)
                push(lambda: (self.buf.at[c], self.buf.at[c], self.recv + 1, (sib, y)), lacks)

        def wait(self):
            @pl.when(y == self.owner)
            def _():
                self.local.wait()

            arrived(self.buf.at[1 - c], self.recv + 1)

    class Pair:
        def __init__(self, device):
            self.device = device
            self.recv = take(1)

        def start(self, ref):
            push(lambda: (ref(), ref(), self.recv, self.device))

        def wait(self, ref):
            arrived(ref, self.recv)

    locals_ = []
    local_count = [0]

    def take_local():
        local_count[0] += 1
        return local_count[0] - 1

    def fetch(source, dest):
        copy = pltpu.make_async_copy(source, dest, lsem.at[take_local()])
        copy.start()
        locals_.append(copy)

    own_lanes = pl.ds(pl.multiple_of(c * 128, 128), 128)
    rows = lambda lo, n: leaf.at[0, pl.ds(lo, n), :]
    b11, b12, b22 = Spread(2, rows(256, 128), s11), Spread(3, rows(256, 128), s12), Spread(3, rows(384, 128), s22)
    bb0, bb1 = Spread(0, rows(256, 256), bq.at[0]), Spread(1, rows(256, 256), bq.at[1])
    be0, be1 = Spread(0, rows(0, 256), e0), Spread(1, rows(128, 128), e1)
    gt, gx1, gx2, gg3 = Gather(tt), Gather(x1), Gather(x2), Gather(g3)
    pimp, phb = Pair((sib, y)), Pair((sib, y))
    fetch(imp, impb.at[c])

    pl.semaphore_wait(barrier, len(greet))
    for piece in (b11, b12, b22, bb0, bb1, be0, be1):
        piece.start()
    push(lambda: (imp, impb.at[c], pimp.recv, (sib, y)))
    push(
        lambda: (src.at[0, :, pl.ds(pl.multiple_of((1 - c) * 128, 128), 128)], hb.at[c], phb.recv, (sib, y))
    )
    fetch(src.at[0, :, own_lanes], hb.at[c])
    fetch(top.at[z, pl.ds(pl.multiple_of(beta * 256 + gamma * 128, 128), 128), own_lanes], tt.at[y, c])
    for h in range(2):
        quarter = pl.ds(pl.multiple_of(h * 256 + gamma * 128, 128), 128)
        fetch(top.at[z, quarter, own_lanes], town.at[pl.ds(h * 128, 128), :])
    fetch(iop.at[0], opv)
    b11.relay()
    b11.wait()
    pimp.wait(impb.at[1 - c])
    for copy in locals_:
        copy.wait()

    hooks = []

    def eliminate(off, last, mid1, mid2, mid3, then):
        def middle():
            mid2()
            side = off()
            w = mm(mb[0], side)
            ws[...] = w
            mb[1] = last() - mm(side, w, TN)

        def end():
            i12 = -mm(ws[...], mb[1])
            sinv[0:128, 0:128] = mb[0] - mm(i12, ws[...], NT)
            sinv[0:128, 128:256] = i12
            sinv[128:256, 0:128] = i12.T
            sinv[128:256, 128:256] = mb[1]
            then()

        hooks.extend([mid1, middle, mid3, end])

    p20, p2s, r2s = Pair((part2, y)), Pair((part2, y)), Pair((sib, y))
    pse2, pee2, ph2 = (Pair((part2, y)) for _ in range(3))
    rse2, ree2 = Pair((sib, y)), Pair((sib, y))
    p30, p3s, r3s, ph3 = Pair((part3, y)), Pair((part3, y)), Pair((sib, y)), Pair((part3, y))
    other = 1 - beta
    across = 1 - gamma
    chunk = lambda who: pl.ds(pl.multiple_of(who * 256, 256), 256)
    lanes = lambda buf, who: jnp.concatenate([buf[who, 0], buf[who, 1]], axis=1)

    ir = lambda k, lo: impb[k, 0:1, lo : lo + 128]

    def mid1():
        b12.relay()
        b22.relay()

    def mid2():
        b12.wait()
        b22.wait()

    def mid3():
        bb0.relay()
        bb1.relay()

    def mid4():
        be0.relay()
        be1.relay()
        gt.start()

    def after1():
        mid4()
        bb0.wait()
        bb1.wait()
        for i, (q, k) in enumerate(((1, 0), (1, 1), (0, 0), (0, 1))):
            bb[:, i * 128 : i * 128 + 128] = bq[q, k]
        inverse, bs = split(sinv[...]), split(bb[:, 0:256])
        xs = mm3(inverse, bs)
        be0.wait()
        be1.wait()
        zs = mm3(bs, split(xs), TN)
        ss2[beta, 0] = e1[0] + diag_of(ir(0, 128)) - zs[0:128, 0:128]
        ss2[beta, 1] = -zs[0:128, 128:256]
        ss2[beta, 2] = e1[1] + diag_of(ir(1, 128)) - zs[128:256, 128:256]
        p20.start(lambda: ss2.at[beta, 0])
        p2s.start(lambda: ss2.at[beta, 1 + c])
        phb.wait(hb.at[1 - c])
        bb[:, 512:640] = hb[0, 256:512, :] + hb[1, 256:512, :]
        xr = mm3(inverse, split(bb[:, 256:640]))
        xrs = split(xr)
        zr = mm3(bs, xrs, TN)
        se2[beta, 0, 0:128, :] = e0[0, 128:256, :] - zr[0:128, 0:128]
        se2[beta, 0, 128:256, :] = -zr[128:256, 0:128]
        se2[beta, 1, 0:128, :] = -zr[0:128, 128:256]
        se2[beta, 1, 128:256, :] = e0[1, 128:256, :] - zr[128:256, 128:256]
        pse2.start(lambda: se2.at[beta, c])
        z1 = mm3(split(bb[:, 384:512]), xrs, TN)
        ee2[beta, 0] = -z1[:, 0:128]
        ee2[beta, 1] = e0[1, 0:128, :] + diag_of(ir(1, 0)) - z1[:, 128:256]
        pee2.start(lambda: ee2.at[beta, c])
        h2[beta, 0:128, :] = hb[0, 128:256, :] - zr[0:128, 256:384]
        h2[beta, 128:256, :] = hb[1, 128:256, :] - zr[128:256, 256:384]
        h2[beta, 256:384, :] = hb[1, 0:128, :] - z1[:, 256:384]
        ph2.start(lambda: h2.at[beta])
        x1[y, c] = xr[:, 256:384]
        gx1.start()

        op_s = split(opv[:, 256:512])
        o0, o1 = opv[:, 0:128], opv[:, 128:256]
        pick = lambda v: jnp.concatenate([jnp.where(c == k, v, jnp.zeros_like(v)) for k in range(2)], axis=1)
        kv2[...] = pick(o1) - mm3(op_s, split(xs))
        k1s[...] = pick(o0) - mm3(op_s, split(xr[:, 0:256]))
        p20.wait(ss2.at[other, 0])
        mb[0] = ss2[0, 0] + ss2[1, 0]

    mb[0] = s11[0] + s11[1] + diag_of(ir(0, 256) + ir(1, 256))
    eliminate(
        lambda: s12[0] + s12[1],
        lambda: s22[0] + s22[1] + diag_of(ir(0, 384) + ir(1, 384)),
        mid1, mid2, mid3, after1,
    )


    def mid1():
        p2s.wait(ss2.at[other, 1 + c])
        r2s.start(lambda: ss2.at[other, 1 + c])
        gt.relay()

    def mid2():
        r2s.wait(ss2.at[other, 2 - c])

    def mid3():
        pse2.wait(se2.at[other, c])
        rse2.start(lambda: se2.at[other, c])

    def after2():
        pee2.wait(ee2.at[other, c])
        ree2.start(lambda: ee2.at[other, c])
        rse2.wait(se2.at[other, 1 - c])
        bb[:, 0:128] = se2[0, 1]
        bb[:, 128:256] = se2[1, 1]
        inverse, bs = split(sinv[...]), split(bb[:, 0:256])
        xs = mm3(inverse, bs)
        ree2.wait(ee2.at[other, 1 - c])
        zs = mm3(bs, split(xs), TN)
        ss3[gamma, 0] = ee2[0, 1] - zs[0:128, 0:128]
        ss3[gamma, 1] = -zs[0:128, 128:256]
        ss3[gamma, 2] = ee2[1, 1] - zs[128:256, 128:256]
        p30.start(lambda: ss3.at[gamma, 0])
        p3s.start(lambda: ss3.at[gamma, 1 + c])
        t0, t1 = split(town[0:128, :]), split(town[128:256, :])
        known_part = mm3(split(se2[0, 0]), t0) + mm3(split(se2[1, 0]), t1)
        h3[gamma, 0:128, :] = mm3(split(ee2[0, 0]), t0)
        h3[gamma, 128:256, :] = mm3(split(ee2[1, 0]), t1)
        ph2.wait(h2.at[other])
        xg = mm3(inverse, split(h2[0, 0:256, :] + h2[1, 0:256, :] + known_part))
        zr = mm3(bs, split(xg), TN)
        h3[gamma, 0:128, :] += h2[0, 256:384, :] - zr[0:128, :]
        h3[gamma, 128:256, :] += h2[1, 256:384, :] - zr[128:256, :]
        ph3.start(lambda: h3.at[gamma])
        x2[y, c] = xg
        gx2.start()
        gx1.relay()

        ko, ki = k1s[:, 0:128], k1s[:, 128:256]
        pick = lambda v: jnp.concatenate([jnp.where(beta == k, v, jnp.zeros_like(v)) for k in range(2)], axis=1)
        k3[...] = pick(ki) - mm3(split(kv2[...]), split(xs))
        gt.wait()
        gx1.wait()
        left = split(jnp.concatenate([ko, -opv[:, 256:512]], axis=1))

        def known(who, carry):
            right = jnp.concatenate([lanes(tt, who), lanes(x1, who)], axis=0)
            out[0, :, chunk(who)] = mm3(left, split(right))
            return carry

        lax.fori_loop(0, 4, known, 0)
        p30.wait(ss3.at[across, 0])
        mb[0] = ss3[0, 0] + ss3[1, 0]

    eliminate(
        lambda: ss2[0, 1] + ss2[1, 1], lambda: ss2[0, 2] + ss2[1, 2], mid1, mid2, mid3, after2
    )


    def mid1():
        p3s.wait(ss3.at[across, 1 + c])
        r3s.start(lambda: ss3.at[across, 1 + c])
        ph3.wait(h3.at[across])
        g3[y, c] = h3[0] + h3[1]
        gg3.start()

    def mid2():
        r3s.wait(ss3.at[across, 2 - c])

    def mid3():
        gx2.relay()

    eliminate(
        lambda: ss3[0, 1] + ss3[1, 1], lambda: ss3[0, 2] + ss3[1, 2],
        mid1, mid2, mid3, lambda: gg3.relay((1, 3)),
    )

    def step(at, carry):
        invert_panel(mb.at[at // 2 % 2], at % 2 * PANEL)
        for k, hook in enumerate(hooks):
            pl.when(at == k)(hook)
        return carry

    lax.fori_loop(0, len(hooks), step, 0)
    k3[...] = -mm3(split(k3[...]), split(sinv[...]))
    gx2.wait()
    left = split(jnp.concatenate([k3[...], kv2[...]], axis=1))
    for d in (0, 1, 3, 2):
        who = (y + d) % 4
        if d == 2:
            gg3.relay((2,))
        gg3.wait((d,))
        right = jnp.concatenate([lanes(g3, who), -lanes(x2, who)], axis=0)
        out[0, :, chunk(who)] += mm3(left, split(right))
    for cond, make in sends:
        if cond is None:
            make().wait_send()
        else:
            pl.when(cond())(lambda make=make: make().wait_send())
    assert count[0] <= NSEM and local_count[0] <= 16


def on_device(leaf_maps, impedance, sources, top_trace, interior_op):
    anywhere = pl.BlockSpec(memory_space=pltpu.HBM)
    vm = lambda *shape: pltpu.VMEM(shape, F32)
    return pl.pallas_call(
        kernel,
        out_shape=jax.ShapeDtypeStruct((1, 256, 1024), F32),
        in_specs=[anywhere] * 5,
        out_specs=pl.BlockSpec(memory_space=pltpu.VMEM),
        scratch_shapes=[
            vm(2, 128, 128), vm(2, 128, 128), vm(2, 128, 128), vm(2, 2, 256, 128), vm(2, 256, 128),
            vm(2, 128, 128), vm(4, 2, 128, 128),
            vm(4, 2, 256, 128), vm(4, 2, 256, 128), vm(4, 2, 256, 128),
            vm(2, 1, 512), vm(2, 512, 128), vm(256, 128), vm(256, 512),
            vm(2, 3, 128, 128), vm(2, 2, 256, 128), vm(2, 2, 128, 128), vm(2, 384, 128),
            vm(2, 3, 128, 128), vm(2, 256, 128),
            vm(2, 128, 128), vm(128, 128), vm(256, 256), vm(256, 640), vm(256, 256),
            vm(256, 256), vm(256, 256),
            pltpu.SemaphoreType.DMA((NSEM,)), pltpu.SemaphoreType.DMA((16,)),
        ],
        compiler_params=pltpu.CompilerParams(
            collective_id=0, has_side_effects=True, vmem_limit_bytes=40 * 2**20
        ),
        name="merge_solve",
    )(*[pltpu.with_memory_space_constraint(a, pltpu.HBM) for a in (leaf_maps, impedance, sources, top_trace, interior_op)])


def solution(mesh):
    return jax.shard_map(
        on_device,
        mesh=mesh,
        in_specs=(
            P("sub", None, "src"),
            P("sub", None),
            P("sub", None, "src"),
            P(None, None, "src"),
            P("sub", "src", None),
        ),
        out_specs=P("sub", "src", None),
        check_vma=False,
    )
```

```python
import jax
import jax.numpy as jnp
from jax import lax
from jax.experimental import pallas as pl
from jax.experimental.pallas import tpu as pltpu
from jax.sharding import PartitionSpec as P

F32 = jnp.float32
MESH = pl.DeviceIdType.MESH
NN = ((1,), (0,))
TN = ((0,), (0,))
NT = ((1,), (1,))
NSEM = 256


def mm(a, b, dims=NN):
    return lax.dot_general(
        a, b, (dims, ((), ())), precision=lax.Precision.HIGHEST, preferred_element_type=F32
    )


def split(a):
    high = a.astype(jnp.bfloat16)
    return high, (a - high.astype(F32)).astype(jnp.bfloat16)


def mm3(a, b, dims=NN):
    dot = lambda p, q: lax.dot_general(p, q, (dims, ((), ())), preferred_element_type=F32)
    return dot(a[0], b[0]) + (dot(a[0], b[1]) + dot(a[1], b[0]))


def tile_steps(panel, at, k):
    lane = lax.broadcasted_iota(jnp.int32, (8, 128), 1)
    row = lax.broadcasted_iota(jnp.int32, (8, 128), 0)
    column = lambda v, j: jnp.take_along_axis(v, jnp.full(v.shape, k + j, jnp.int32), axis=1)
    spread = lambda v, i: jnp.broadcast_to(v[i : i + 1, :], (8, 128))
    tile = panel[at]
    cols = [column(tile, j) for j in range(8)]
    others = {u: [column(panel[u], j) for j in range(8)] for u in range(len(panel)) if u != at}
    for q in range(0, 8, 2):
        a, b, d = spread(cols[q], q), spread(cols[q + 1], q), spread(cols[q + 1], q + 1)
        r = 1.0 / (a * d - b * b)
        i00, i01, i11 = d * r, -(b * r), a * r
        pivots = (row >= q) & (row < q + 2)
        m0 = jnp.where(pivots, jnp.where(row == q, -1.0, 0.0), cols[q])
        m1 = jnp.where(pivots, jnp.where(row == q + 1, -1.0, 0.0), cols[q + 1])

        def change(t0, t1):
            return m0 * (i00 * t0 + i01 * t1) + m1 * (i01 * t0 + i11 * t1)

        for j in range(q + 2, 8):
            cols[j] = jnp.where(pivots, 0.0, cols[j]) - change(spread(cols[j], q), spread(cols[j], q + 1))
        l0, l1 = lane == k + q, lane == k + q + 1
        t0 = jnp.where(l0, 1.0, jnp.where(l1, 0.0, spread(tile, q)))
        t1 = jnp.where(l1, 1.0, jnp.where(l0, 0.0, spread(tile, q + 1)))
        tile = jnp.where(pivots | l0 | l1, 0.0, tile) - change(t0, t1)
    rows = [spread(tile, j) for j in range(8)]
    done = (lane >= k) & (lane < k + 8)

    def follow(u):
        terms = [x * r for x, r in zip(others[u], rows)]
        while len(terms) > 1:
            terms = [terms[i] + terms[i + 1] for i in range(0, len(terms), 2)]
        return jnp.where(done, 0.0, panel[u]) - terms[0]

    return [tile if u == at else follow(u) for u in range(len(panel))]


PANEL = 64


def invert_panel(m, r0):
    n = m.shape[0]
    lane = lax.broadcasted_iota(jnp.int32, (n, n), 1)
    r0 = pl.multiple_of(r0, PANEL)
    whole = m[...]
    tiles = [pl.ds(pl.multiple_of(r0 + 8 * i, 8), 8) for i in range(PANEL // 8)]
    panel = [m[i, :] for i in tiles]
    for at in range(PANEL // 8):
        panel = tile_steps(panel, at, r0 + 8 * at)
    inside = (lane >= r0) & (lane < r0 + PANEL)
    rows = jnp.concatenate(panel * (n // PANEL), axis=0)
    m[...] = jnp.where(inside, 0.0, whole) - mm(jnp.where(inside, whole, 0.0), rows)
    for i, tile in zip(tiles, panel):
        m[i, :] = tile


def diag_of(row):
    n = row.shape[1]
    here = lax.broadcasted_iota(jnp.int32, (n, n), 0) == lax.broadcasted_iota(jnp.int32, (n, n), 1)
    return jnp.where(here, row, 0.0)


def kernel(
    leaf, imp, src, top, iop, out,
    s11, s12, s22, bq, e0, e1, tt, x1, x2, g3, impb, hb, town, opv,
    ss2, se2, ee2, h2, ss3, h3,
    mb, ws, sinv, bb, k1s, kv2, k3, sem, lsem,
):
    s = lax.axis_index("sub")
    y = lax.axis_index("src")
    c = s % 2
    x = s // 2 % 4
    z = s // 8
    beta = x % 2
    gamma = x // 2
    sib = s + 1 - 2 * c
    part2 = z * 8 + (x + 1 - 2 * beta) * 2 + c
    part3 = z * 8 + (3 - x) * 2 + c

    barrier = pltpu.get_barrier_semaphore()
    greet = [(s, (y + d) % 4) for d in (1, 2, 3)] + [(sib, y), (part2, y), (part3, y)]
    for device in greet:
        pl.semaphore_signal(barrier, inc=1, device_id=device, device_id_type=MESH)

    count = [0]
    sends = []

    def take(n):
        base = count[0]
        count[0] += n
        return base

    def push(get, cond=None):
        sent = take(1)

        def make():
            source, dest, recv, device = get()
            return pltpu.make_async_remote_copy(
                source, dest, sem.at[sent], sem.at[recv], device_id=device, device_id_type=MESH
            )

        make().start()
        sends.append((cond, make))

    def arrived(ref, recv):
        pltpu.make_async_remote_copy(
            ref, ref, sem.at[0], sem.at[recv], device_id=(sib, y), device_id_type=MESH
        ).wait_recv()

    class Gather:
        def __init__(self, buf):
            self.buf = buf
            self.recv = take(8)

        def start(self):
            def to(device):
                mine = self.buf.at[y, c]
                return mine, mine, self.recv + y * 2 + c, device

            for d in (1, 3, 2):
                push(lambda d=d: to((s, (y + d) % 4)))
            push(lambda: to((sib, y)))

        def relay(self, steps=(1, 3, 2)):
            def onward(d):
                who = (y + d) % 4
                slot = self.buf.at[who, c]
                return slot, slot, self.recv + who * 2 + c, (sib, y)

            for d in steps:
                slot, _, recv, _ = onward(d)
                arrived(slot, recv)
                push(lambda d=d: onward(d))

        def wait(self, steps=(0, 1, 3, 2)):
            for d in steps:
                who = (y + d) % 4
                arrived(self.buf.at[who, 1 - c], self.recv + who * 2 + 1 - c)

    class Spread:
        def __init__(self, owner, source, buf):
            self.owner, self.source, self.buf = owner, source, buf
            self.recv = take(2)
            self.local = pltpu.make_async_copy(source, buf.at[c], lsem.at[take_local()])

        def start(self):
            owns = lambda: y == self.owner

            @pl.when(owns())
            def _():
                self.local.start()
                for d in (1, 3, 2):
                    there = (self.owner + d) % 4
                    push(lambda there=there: (self.source, self.buf.at[c], self.recv, (s, there)), owns)
                push(lambda: (self.source, self.buf.at[c], self.recv + 1, (sib, y)), owns)

        def relay(self):
            lacks = lambda: y != self.owner

            @pl.when(lacks())
            def _():
                arrived(self.buf.at[c], self.recv)
                push(lambda: (self.buf.at[c], self.buf.at[c], self.recv + 1, (sib, y)), lacks)

        def wait(self):
            @pl.when(y == self.owner)
            def _():
                self.local.wait()

            arrived(self.buf.at[1 - c], self.recv + 1)

    class Pair:
        def __init__(self, device):
            self.device = device
            self.recv = take(1)

        def start(self, ref):
            push(lambda: (ref(), ref(), self.recv, self.device))

        def wait(self, ref):
            arrived(ref, self.recv)

    locals_ = []
    local_count = [0]

    def take_local():
        local_count[0] += 1
        return local_count[0] - 1

    def fetch(source, dest):
        copy = pltpu.make_async_copy(source, dest, lsem.at[take_local()])
        copy.start()
        locals_.append(copy)

    own_lanes = pl.ds(pl.multiple_of(c * 128, 128), 128)
    rows = lambda lo, n: leaf.at[0, pl.ds(lo, n), :]
    b11, b12, b22 = Spread(2, rows(256, 128), s11), Spread(3, rows(256, 128), s12), Spread(3, rows(384, 128), s22)
    bb0, bb1 = Spread(0, rows(256, 256), bq.at[0]), Spread(1, rows(256, 256), bq.at[1])
    be0, be1 = Spread(0, rows(0, 256), e0), Spread(1, rows(128, 128), e1)
    gt, gx1, gx2, gg3 = Gather(tt), Gather(x1), Gather(x2), Gather(g3)
    pimp, phb = Pair((sib, y)), Pair((sib, y))
    fetch(imp, impb.at[c])

    pl.semaphore_wait(barrier, len(greet))
    for piece in (b11, b12, b22, bb0, bb1, be0, be1):
        piece.start()
    push(lambda: (imp, impb.at[c], pimp.recv, (sib, y)))
    push(
        lambda: (src.at[0, :, pl.ds(pl.multiple_of((1 - c) * 128, 128), 128)], hb.at[c], phb.recv, (sib, y))
    )
    fetch(src.at[0, :, own_lanes], hb.at[c])
    fetch(top.at[z, pl.ds(pl.multiple_of(beta * 256 + gamma * 128, 128), 128), own_lanes], tt.at[y, c])
    for h in range(2):
        quarter = pl.ds(pl.multiple_of(h * 256 + gamma * 128, 128), 128)
        fetch(top.at[z, quarter, own_lanes], town.at[pl.ds(h * 128, 128), :])
    fetch(iop.at[0], opv)
    b11.relay()
    b11.wait()
    pimp.wait(impb.at[1 - c])
    for copy in locals_:
        copy.wait()

    hooks = []

    def eliminate(off, last, mid1, mid2, mid3, then):
        def middle():
            mid2()
            side = off()
            w = mm(mb[0], side)
            ws[...] = w
            mb[1] = last() - mm(side, w, TN)

        def end():
            i12 = -mm(ws[...], mb[1])
            sinv[0:128, 0:128] = mb[0] - mm(i12, ws[...], NT)
            sinv[0:128, 128:256] = i12
            sinv[128:256, 0:128] = i12.T
            sinv[128:256, 128:256] = mb[1]
            then()

        hooks.extend([mid1, middle, mid3, end])

    p20, p2s, r2s = Pair((part2, y)), Pair((part2, y)), Pair((sib, y))
    pse2, pee2, ph2 = (Pair((part2, y)) for _ in range(3))
    rse2, ree2 = Pair((sib, y)), Pair((sib, y))
    p30, p3s, r3s, ph3 = Pair((part3, y)), Pair((part3, y)), Pair((sib, y)), Pair((part3, y))
    other = 1 - beta
    across = 1 - gamma
    chunk = lambda who: pl.ds(pl.multiple_of(who * 256, 256), 256)
    lanes = lambda buf, who: jnp.concatenate([buf[who, 0], buf[who, 1]], axis=1)

    ir = lambda k, lo: impb[k, 0:1, lo : lo + 128]

    def mid1():
        b12.relay()
        b22.relay()

    def mid2():
        b12.wait()
        b22.wait()

    def mid3():
        bb0.relay()
        bb1.relay()

    def mid4():
        be0.relay()
        be1.relay()
        gt.start()

    def after1():
        mid4()
        bb0.wait()
        bb1.wait()
        for i, (q, k) in enumerate(((1, 0), (1, 1), (0, 0), (0, 1))):
            bb[:, i * 128 : i * 128 + 128] = bq[q, k]
        inverse, bs = split(sinv[...]), split(bb[:, 0:256])
        xs = mm3(inverse, bs)
        be0.wait()
        be1.wait()
        zs = mm3(bs, split(xs), TN)
        ss2[beta, 0] = e1[0] + diag_of(ir(0, 128)) - zs[0:128, 0:128]
        ss2[beta, 1] = -zs[0:128, 128:256]
        ss2[beta, 2] = e1[1] + diag_of(ir(1, 128)) - zs[128:256, 128:256]
        p20.start(lambda: ss2.at[beta, 0])
        p2s.start(lambda: ss2.at[beta, 1 + c])
        phb.wait(hb.at[1 - c])
        bb[:, 512:640] = hb[0, 256:512, :] + hb[1, 256:512, :]
        xr = mm3(inverse, split(bb[:, 256:640]))
        xrs = split(xr)
        zr = mm3(bs, xrs, TN)
        se2[beta, 0, 0:128, :] = e0[0, 128:256, :] - zr[0:128, 0:128]
        se2[beta, 0, 128:256, :] = -zr[128:256, 0:128]
        se2[beta, 1, 0:128, :] = -zr[0:128, 128:256]
        se2[beta, 1, 128:256, :] = e0[1, 128:256, :] - zr[128:256, 128:256]
        pse2.start(lambda: se2.at[beta, c])
        z1 = mm3(split(bb[:, 384:512]), xrs, TN)
        ee2[beta, 0] = -z1[:, 0:128]
        ee2[beta, 1] = e0[1, 0:128, :] + diag_of(ir(1, 0)) - z1[:, 128:256]
        pee2.start(lambda: ee2.at[beta, c])
        h2[beta, 0:128, :] = hb[0, 128:256, :] - zr[0:128, 256:384]
        h2[beta, 128:256, :] = hb[1, 128:256, :] - zr[128:256, 256:384]
        h2[beta, 256:384, :] = hb[1, 0:128, :] - z1[:, 256:384]
        ph2.start(lambda: h2.at[beta])
        x1[y, c] = xr[:, 256:384]
        gx1.start()

        op_s = split(opv[:, 256:512])
        o0, o1 = opv[:, 0:128], opv[:, 128:256]
        pick = lambda v: jnp.concatenate([jnp.where(c == k, v, jnp.zeros_like(v)) for k in range(2)], axis=1)
        kv2[...] = pick(o1) - mm3(op_s, split(xs))
        k1s[...] = pick(o0) - mm3(op_s, split(xr[:, 0:256]))
        p20.wait(ss2.at[other, 0])
        mb[0] = ss2[0, 0] + ss2[1, 0]

    mb[0] = s11[0] + s11[1] + diag_of(ir(0, 256) + ir(1, 256))
    eliminate(
        lambda: s12[0] + s12[1],
        lambda: s22[0] + s22[1] + diag_of(ir(0, 384) + ir(1, 384)),
        mid1, mid2, mid3, after1,
    )


    def mid1():
        p2s.wait(ss2.at[other, 1 + c])
        r2s.start(lambda: ss2.at[other, 1 + c])

    def mid2():
        r2s.wait(ss2.at[other, 2 - c])

    def mid3():
        pse2.wait(se2.at[other, c])
        rse2.start(lambda: se2.at[other, c])
        gt.relay()

    def after2():
        pee2.wait(ee2.at[other, c])
        ree2.start(lambda: ee2.at[other, c])
        rse2.wait(se2.at[other, 1 - c])
        bb[:, 0:128] = se2[0, 1]
        bb[:, 128:256] = se2[1, 1]
        inverse, bs = split(sinv[...]), split(bb[:, 0:256])
        xs = mm3(inverse, bs)
        ree2.wait(ee2.at[other, 1 - c])
        zs = mm3(bs, split(xs), TN)
        ss3[gamma, 0] = ee2[0, 1] - zs[0:128, 0:128]
        ss3[gamma, 1] = -zs[0:128, 128:256]
        ss3[gamma, 2] = ee2[1, 1] - zs[128:256, 128:256]
        p30.start(lambda: ss3.at[gamma, 0])
        t0, t1 = split(town[0:128, :]), split(town[128:256, :])
        known_part = mm3(split(se2[0, 0]), t0) + mm3(split(se2[1, 0]), t1)
        h3[gamma, 0:128, :] = mm3(split(ee2[0, 0]), t0)
        h3[gamma, 128:256, :] = mm3(split(ee2[1, 0]), t1)
        ph2.wait(h2.at[other])
        xg = mm3(inverse, split(h2[0, 0:256, :] + h2[1, 0:256, :] + known_part))
        zr = mm3(bs, split(xg), TN)
        h3[gamma, 0:128, :] += h2[0, 256:384, :] - zr[0:128, :]
        h3[gamma, 128:256, :] += h2[1, 256:384, :] - zr[128:256, :]
        ph3.start(lambda: h3.at[gamma])
        p3s.start(lambda: ss3.at[gamma, 1 + c])
        x2[y, c] = xg
        gx2.start()
        gx1.relay()

        ko, ki = k1s[:, 0:128], k1s[:, 128:256]
        pick = lambda v: jnp.concatenate([jnp.where(beta == k, v, jnp.zeros_like(v)) for k in range(2)], axis=1)
        k3[...] = pick(ki) - mm3(split(kv2[...]), split(xs))
        gt.wait()
        gx1.wait()
        left = split(jnp.concatenate([ko, -opv[:, 256:512]], axis=1))

        def known(who, carry):
            right = jnp.concatenate([lanes(tt, who), lanes(x1, who)], axis=0)
            out[0, :, chunk(who)] = mm3(left, split(right))
            return carry

        lax.fori_loop(0, 4, known, 0)
        p30.wait(ss3.at[across, 0])
        mb[0] = ss3[0, 0] + ss3[1, 0]

    eliminate(
        lambda: ss2[0, 1] + ss2[1, 1], lambda: ss2[0, 2] + ss2[1, 2], mid1, mid2, mid3, after2
    )


    def mid1():
        ph3.wait(h3.at[across])
        g3[y, c] = h3[0] + h3[1]
        gg3.start()

    def mid2():
        p3s.wait(ss3.at[across, 1 + c])
        r3s.start(lambda: ss3.at[across, 1 + c])
        r3s.wait(ss3.at[across, 2 - c])

    def mid3():
        gx2.relay()

    eliminate(
        lambda: ss3[0, 1] + ss3[1, 1], lambda: ss3[0, 2] + ss3[1, 2],
        mid1, mid2, mid3, lambda: gg3.relay((1, 3)),
    )

    def step(at, carry):
        invert_panel(mb.at[at // 2 % 2], at % 2 * PANEL)
        for k, hook in enumerate(hooks):
            pl.when(at == k)(hook)
        return carry

    lax.fori_loop(0, len(hooks), step, 0)
    k3[...] = -mm3(split(k3[...]), split(sinv[...]))
    gx2.wait()
    left = split(jnp.concatenate([k3[...], kv2[...]], axis=1))
    for d in (0, 1, 3, 2):
        who = (y + d) % 4
        if d == 2:
            gg3.relay((2,))
        gg3.wait((d,))
        right = jnp.concatenate([lanes(g3, who), -lanes(x2, who)], axis=0)
        out[0, :, chunk(who)] += mm3(left, split(right))
    for cond, make in sends:
        if cond is None:
            make().wait_send()
        else:
            pl.when(cond())(lambda make=make: make().wait_send())
    assert count[0] <= NSEM and local_count[0] <= 16


def on_device(leaf_maps, impedance, sources, top_trace, interior_op):
    anywhere = pl.BlockSpec(memory_space=pltpu.HBM)
    vm = lambda *shape: pltpu.VMEM(shape, F32)
    return pl.pallas_call(
        kernel,
        out_shape=jax.ShapeDtypeStruct((1, 256, 1024), F32),
        in_specs=[anywhere] * 5,
        out_specs=pl.BlockSpec(memory_space=pltpu.VMEM),
        scratch_shapes=[
            vm(2, 128, 128), vm(2, 128, 128), vm(2, 128, 128), vm(2, 2, 256, 128), vm(2, 256, 128),
            vm(2, 128, 128), vm(4, 2, 128, 128),
            vm(4, 2, 256, 128), vm(4, 2, 256, 128), vm(4, 2, 256, 128),
            vm(2, 1, 512), vm(2, 512, 128), vm(256, 128), vm(256, 512),
            vm(2, 3, 128, 128), vm(2, 2, 256, 128), vm(2, 2, 128, 128), vm(2, 384, 128),
            vm(2, 3, 128, 128), vm(2, 256, 128),
            vm(2, 128, 128), vm(128, 128), vm(256, 256), vm(256, 640), vm(256, 256),
            vm(256, 256), vm(256, 256),
            pltpu.SemaphoreType.DMA((NSEM,)), pltpu.SemaphoreType.DMA((16,)),
        ],
        compiler_params=pltpu.CompilerParams(
            collective_id=0, has_side_effects=True, vmem_limit_bytes=40 * 2**20
        ),
        name="merge_solve",
    )(*[pltpu.with_memory_space_constraint(a, pltpu.HBM) for a in (leaf_maps, impedance, sources, top_trace, interior_op)])


def solution(mesh):
    return jax.shard_map(
        on_device,
        mesh=mesh,
        in_specs=(
            P("sub", None, "src"),
            P("sub", None),
            P("sub", None, "src"),
            P(None, None, "src"),
            P("sub", "src", None),
        ),
        out_specs=P("sub", "src", None),
        check_vma=False,
    )
```

```python
import jax
import jax.numpy as jnp
from jax import lax
from jax.experimental import pallas as pl
from jax.experimental.pallas import tpu as pltpu
from jax.sharding import PartitionSpec as P

F32 = jnp.float32
MESH = pl.DeviceIdType.MESH
NN = ((1,), (0,))
TN = ((0,), (0,))
NT = ((1,), (1,))
NSEM = 256


def mm(a, b, dims=NN):
    return lax.dot_general(
        a, b, (dims, ((), ())), precision=lax.Precision.HIGHEST, preferred_element_type=F32
    )


def split(a):
    high = a.astype(jnp.bfloat16)
    return high, (a - high.astype(F32)).astype(jnp.bfloat16)


def mm3(a, b, dims=NN):
    dot = lambda p, q: lax.dot_general(p, q, (dims, ((), ())), preferred_element_type=F32)
    return dot(a[0], b[0]) + (dot(a[0], b[1]) + dot(a[1], b[0]))


def tile_steps(panel, at, k):
    lane = lax.broadcasted_iota(jnp.int32, (8, 128), 1)
    row = lax.broadcasted_iota(jnp.int32, (8, 128), 0)
    column = lambda v, j: jnp.take_along_axis(v, jnp.full(v.shape, k + j, jnp.int32), axis=1)
    spread = lambda v, i: jnp.broadcast_to(v[i : i + 1, :], (8, 128))
    tile = panel[at]
    cols = [column(tile, j) for j in range(8)]
    others = {u: [column(panel[u], j) for j in range(8)] for u in range(len(panel)) if u != at}
    for q in range(0, 8, 2):
        a, b, d = spread(cols[q], q), spread(cols[q + 1], q), spread(cols[q + 1], q + 1)
        r = 1.0 / (a * d - b * b)
        i00, i01, i11 = d * r, -(b * r), a * r
        pivots = (row >= q) & (row < q + 2)
        m0 = jnp.where(pivots, jnp.where(row == q, -1.0, 0.0), cols[q])
        m1 = jnp.where(pivots, jnp.where(row == q + 1, -1.0, 0.0), cols[q + 1])

        def change(t0, t1):
            return m0 * (i00 * t0 + i01 * t1) + m1 * (i01 * t0 + i11 * t1)

        for j in range(q + 2, 8):
            cols[j] = jnp.where(pivots, 0.0, cols[j]) - change(spread(cols[j], q), spread(cols[j], q + 1))
        l0, l1 = lane == k + q, lane == k + q + 1
        t0 = jnp.where(l0, 1.0, jnp.where(l1, 0.0, spread(tile, q)))
        t1 = jnp.where(l1, 1.0, jnp.where(l0, 0.0, spread(tile, q + 1)))
        tile = jnp.where(pivots | l0 | l1, 0.0, tile) - change(t0, t1)
    rows = [spread(tile, j) for j in range(8)]
    done = (lane >= k) & (lane < k + 8)

    def follow(u):
        terms = [x * r for x, r in zip(others[u], rows)]
        while len(terms) > 1:
            terms = [terms[i] + terms[i + 1] for i in range(0, len(terms), 2)]
        return jnp.where(done, 0.0, panel[u]) - terms[0]

    return [tile if u == at else follow(u) for u in range(len(panel))]


PANEL = 64


def invert_panel(m, r0):
    n = m.shape[0]
    lane = lax.broadcasted_iota(jnp.int32, (n, n), 1)
    r0 = pl.multiple_of(r0, PANEL)
    whole = m[...]
    tiles = [pl.ds(pl.multiple_of(r0 + 8 * i, 8), 8) for i in range(PANEL // 8)]
    panel = [m[i, :] for i in tiles]
    for at in range(PANEL // 8):
        panel = tile_steps(panel, at, r0 + 8 * at)
    inside = (lane >= r0) & (lane < r0 + PANEL)
    rows = jnp.concatenate(panel * (n // PANEL), axis=0)
    m[...] = jnp.where(inside, 0.0, whole) - mm(jnp.where(inside, whole, 0.0), rows)
    for i, tile in zip(tiles, panel):
        m[i, :] = tile


def diag_of(row):
    n = row.shape[1]
    here = lax.broadcasted_iota(jnp.int32, (n, n), 0) == lax.broadcasted_iota(jnp.int32, (n, n), 1)
    return jnp.where(here, row, 0.0)


def kernel(
    leaf, imp, src, top, iop, out,
    s11, s12, s22, bq, e0, e1, tt, x1, x2, g3, impb, hb, town, opv,
    ss2, se2, ee2, h2, ss3, h3,
    mb, ws, sinv, bb, k1s, kv2, k3, sem, lsem,
):
    s = lax.axis_index("sub")
    y = lax.axis_index("src")
    c = s % 2
    x = s // 2 % 4
    z = s // 8
    beta = x % 2
    gamma = x // 2
    sib = s + 1 - 2 * c
    part2 = z * 8 + (x + 1 - 2 * beta) * 2 + c
    part3 = z * 8 + (3 - x) * 2 + c

    barrier = pltpu.get_barrier_semaphore()
    greet = [(s, (y + d) % 4) for d in (1, 2, 3)] + [(sib, y), (part2, y), (part3, y)]
    for device in greet:
        pl.semaphore_signal(barrier, inc=1, device_id=device, device_id_type=MESH)

    count = [0]
    sends = []

    def take(n):
        base = count[0]
        count[0] += n
        return base

    def push(get, cond=None):
        sent = take(1)

        def make():
            source, dest, recv, device = get()
            return pltpu.make_async_remote_copy(
                source, dest, sem.at[sent], sem.at[recv], device_id=device, device_id_type=MESH
            )

        make().start()
        sends.append((cond, make))

    def arrived(ref, recv):
        pltpu.make_async_remote_copy(
            ref, ref, sem.at[0], sem.at[recv], device_id=(sib, y), device_id_type=MESH
        ).wait_recv()

    class Gather:
        def __init__(self, buf):
            self.buf = buf
            self.recv = take(8)

        def start(self):
            def to(device):
                mine = self.buf.at[y, c]
                return mine, mine, self.recv + y * 2 + c, device

            for d in (1, 3, 2):
                push(lambda d=d: to((s, (y + d) % 4)))
            push(lambda: to((sib, y)))

        def relay(self, steps=(1, 3, 2)):
            def onward(d):
                who = (y + d) % 4
                slot = self.buf.at[who, c]
                return slot, slot, self.recv + who * 2 + c, (sib, y)

            for d in steps:
                slot, _, recv, _ = onward(d)
                arrived(slot, recv)
                push(lambda d=d: onward(d))

        def wait(self, steps=(0, 1, 3, 2)):
            for d in steps:
                who = (y + d) % 4
                arrived(self.buf.at[who, 1 - c], self.recv + who * 2 + 1 - c)

    class Spread:
        def __init__(self, owner, source, buf, core=None):
            self.mine = lambda: True if core is None else c == core
            self.core = core
            self.owner, self.source, self.buf = owner, source, buf
            self.recv = take(2)
            self.local = pltpu.make_async_copy(source, buf.at[c], lsem.at[take_local()])

        def start(self):
            owns = lambda: (y == self.owner) & self.mine()

            @pl.when(owns())
            def _():
                self.local.start()
                for d in (1, 3, 2):
                    there = (self.owner + d) % 4
                    push(lambda there=there: (self.source, self.buf.at[c], self.recv, (s, there)), owns)
                push(lambda: (self.source, self.buf.at[c], self.recv + 1, (sib, y)), owns)

        def relay(self):
            lacks = lambda: (y != self.owner) & self.mine()

            @pl.when(lacks())
            def _():
                arrived(self.buf.at[c], self.recv)
                push(lambda: (self.buf.at[c], self.buf.at[c], self.recv + 1, (sib, y)), lacks)

        def wait(self):
            pl.when((y == self.owner) & self.mine())(self.local.wait)
            other = lambda: arrived(self.buf.at[1 - c], self.recv + 1)
            other() if self.core is None else pl.when(c != self.core)(other)

    class Pair:
        def __init__(self, device):
            self.device = device
            self.recv = take(1)

        def start(self, ref):
            push(lambda: (ref(), ref(), self.recv, self.device))

        def wait(self, ref):
            arrived(ref, self.recv)

    locals_ = []
    local_count = [0]

    def take_local():
        local_count[0] += 1
        return local_count[0] - 1

    def fetch(source, dest):
        copy = pltpu.make_async_copy(source, dest, lsem.at[take_local()])
        copy.start()
        locals_.append(copy)

    own_lanes = pl.ds(pl.multiple_of(c * 128, 128), 128)
    rows = lambda lo, n: leaf.at[0, pl.ds(lo, n), :]
    b11, b12, b22 = Spread(2, rows(256, 128), s11), Spread(3, rows(256, 128), s12), Spread(3, rows(384, 128), s22)
    bb0, bb1 = Spread(0, rows(256, 256), bq.at[0]), Spread(1, rows(256, 256), bq.at[1])
    low, high = pl.ds(0, 128), pl.ds(128, 128)
    be0, be1 = Spread(0, rows(128, 128), e0.at[:, high]), Spread(1, rows(128, 128), e1)
    be2 = Spread(0, rows(0, 128), e0.at[:, low], 1)
    gt, gx1, gx2, gg3 = Gather(tt), Gather(x1), Gather(x2), Gather(g3)
    pimp, phb = Pair((sib, y)), Pair((sib, y))
    fetch(imp, impb.at[c])

    pl.semaphore_wait(barrier, len(greet))
    for piece in (b11, b12, b22, bb0, bb1, be0, be1, be2):
        piece.start()
    push(lambda: (imp, impb.at[c], pimp.recv, (sib, y)))
    push(
        lambda: (src.at[0, :, pl.ds(pl.multiple_of((1 - c) * 128, 128), 128)], hb.at[c], phb.recv, (sib, y))
    )
    fetch(src.at[0, :, own_lanes], hb.at[c])
    fetch(top.at[z, pl.ds(pl.multiple_of(beta * 256 + gamma * 128, 128), 128), own_lanes], tt.at[y, c])
    for h in range(2):
        quarter = pl.ds(pl.multiple_of(h * 256 + gamma * 128, 128), 128)
        fetch(top.at[z, quarter, own_lanes], town.at[pl.ds(h * 128, 128), :])
    fetch(iop.at[0], opv)
    b11.relay()
    b11.wait()
    pimp.wait(impb.at[1 - c])
    for copy in locals_:
        copy.wait()

    hooks = []

    def eliminate(off, last, mid1, mid2, mid3, then):
        def middle():
            mid2()
            side = off()
            w = mm(mb[0], side)
            ws[...] = w
            mb[1] = last() - mm(side, w, TN)

        def end():
            i12 = -mm(ws[...], mb[1])
            sinv[0:128, 0:128] = mb[0] - mm(i12, ws[...], NT)
            sinv[0:128, 128:256] = i12
            sinv[128:256, 0:128] = i12.T
            sinv[128:256, 128:256] = mb[1]
            then()

        hooks.extend([mid1, middle, mid3, end])

    p20, p2s, r2s = Pair((part2, y)), Pair((part2, y)), Pair((sib, y))
    pse2, pee2, ph2 = (Pair((part2, y)) for _ in range(3))
    rse2, ree2 = Pair((sib, y)), Pair((sib, y))
    p30, p3s, r3s, ph3 = Pair((part3, y)), Pair((part3, y)), Pair((sib, y)), Pair((part3, y))
    other = 1 - beta
    across = 1 - gamma
    chunk = lambda who: pl.ds(pl.multiple_of(who * 256, 256), 256)
    lanes = lambda buf, who: jnp.concatenate([buf[who, 0], buf[who, 1]], axis=1)

    ir = lambda k, lo: impb[k, 0:1, lo : lo + 128]

    def mid1():
        b12.relay()
        b22.relay()

    def mid2():
        b12.wait()
        b22.wait()

    def mid3():
        bb0.relay()
        bb1.relay()

    def mid4():
        be0.relay()
        be1.relay()
        be2.relay()
        gt.start()

    def after1():
        mid4()
        bb0.wait()
        bb1.wait()
        for i, (q, k) in enumerate(((1, 0), (1, 1), (0, 0), (0, 1))):
            bb[:, i * 128 : i * 128 + 128] = bq[q, k]
        inverse, bs = split(sinv[...]), split(bb[:, 0:256])
        xs = mm3(inverse, bs)
        be0.wait()
        be1.wait()
        be2.wait()
        zs = mm3(bs, split(xs), TN)
        ss2[beta, 0] = e1[0] + diag_of(ir(0, 128)) - zs[0:128, 0:128]
        ss2[beta, 1] = -zs[0:128, 128:256]
        ss2[beta, 2] = e1[1] + diag_of(ir(1, 128)) - zs[128:256, 128:256]
        p20.start(lambda: ss2.at[beta, 0])
        p2s.start(lambda: ss2.at[beta, 1 + c])
        phb.wait(hb.at[1 - c])
        bb[:, 512:640] = hb[0, 256:512, :] + hb[1, 256:512, :]
        xr = mm3(inverse, split(bb[:, 256:640]))
        xrs = split(xr)
        zr = mm3(bs, xrs, TN)
        se2[beta, 0, 0:128, :] = e0[0, 128:256, :] - zr[0:128, 0:128]
        se2[beta, 0, 128:256, :] = -zr[128:256, 0:128]
        se2[beta, 1, 0:128, :] = -zr[0:128, 128:256]
        se2[beta, 1, 128:256, :] = e0[1, 128:256, :] - zr[128:256, 128:256]
        pse2.start(lambda: se2.at[beta, c])
        z1 = mm3(split(bb[:, 384:512]), xrs, TN)
        ee2[beta, 0] = -z1[:, 0:128]
        ee2[beta, 1] = e0[1, 0:128, :] + diag_of(ir(1, 0)) - z1[:, 128:256]
        pee2.start(lambda: ee2.at[beta, c])
        h2[beta, 0:128, :] = hb[0, 128:256, :] - zr[0:128, 256:384]
        h2[beta, 128:256, :] = hb[1, 128:256, :] - zr[128:256, 256:384]
        h2[beta, 256:384, :] = hb[1, 0:128, :] - z1[:, 256:384]
        ph2.start(lambda: h2.at[beta])
        x1[y, c] = xr[:, 256:384]
        gx1.start()

        op_s = split(opv[:, 256:512])
        o0, o1 = opv[:, 0:128], opv[:, 128:256]
        pick = lambda v: jnp.concatenate([jnp.where(c == k, v, jnp.zeros_like(v)) for k in range(2)], axis=1)
        kv2[...] = pick(o1) - mm3(op_s, split(xs))
        k1s[...] = pick(o0) - mm3(op_s, split(xr[:, 0:256]))
        p20.wait(ss2.at[other, 0])
        mb[0] = ss2[0, 0] + ss2[1, 0]

    mb[0] = s11[0] + s11[1] + diag_of(ir(0, 256) + ir(1, 256))
    eliminate(
        lambda: s12[0] + s12[1],
        lambda: s22[0] + s22[1] + diag_of(ir(0, 384) + ir(1, 384)),
        mid1, mid2, mid3, after1,
    )


    def mid1():
        p2s.wait(ss2.at[other, 1 + c])
        r2s.start(lambda: ss2.at[other, 1 + c])

    def mid2():
        r2s.wait(ss2.at[other, 2 - c])

    def mid3():
        pse2.wait(se2.at[other, c])
        rse2.start(lambda: se2.at[other, c])
        gt.relay()

    def after2():
        pee2.wait(ee2.at[other, c])
        ree2.start(lambda: ee2.at[other, c])
        rse2.wait(se2.at[other, 1 - c])
        bb[:, 0:128] = se2[0, 1]
        bb[:, 128:256] = se2[1, 1]
        inverse, bs = split(sinv[...]), split(bb[:, 0:256])
        xs = mm3(inverse, bs)
        ree2.wait(ee2.at[other, 1 - c])
        zs = mm3(bs, split(xs), TN)
        ss3[gamma, 0] = ee2[0, 1] - zs[0:128, 0:128]
        ss3[gamma, 1] = -zs[0:128, 128:256]
        ss3[gamma, 2] = ee2[1, 1] - zs[128:256, 128:256]
        p30.start(lambda: ss3.at[gamma, 0])
        t0, t1 = split(town[0:128, :]), split(town[128:256, :])
        known_part = mm3(split(se2[0, 0]), t0) + mm3(split(se2[1, 0]), t1)
        h3[gamma, 0:128, :] = mm3(split(ee2[0, 0]), t0)
        h3[gamma, 128:256, :] = mm3(split(ee2[1, 0]), t1)
        ph2.wait(h2.at[other])
        xg = mm3(inverse, split(h2[0, 0:256, :] + h2[1, 0:256, :] + known_part))
        zr = mm3(bs, split(xg), TN)
        h3[gamma, 0:128, :] += h2[0, 256:384, :] - zr[0:128, :]
        h3[gamma, 128:256, :] += h2[1, 256:384, :] - zr[128:256, :]
        ph3.start(lambda: h3.at[gamma])
        p3s.start(lambda: ss3.at[gamma, 1 + c])
        x2[y, c] = xg
        gx2.start()
        gx1.relay()

        ko, ki = k1s[:, 0:128], k1s[:, 128:256]
        pick = lambda v: jnp.concatenate([jnp.where(beta == k, v, jnp.zeros_like(v)) for k in range(2)], axis=1)
        k3[...] = pick(ki) - mm3(split(kv2[...]), split(xs))
        gt.wait()
        gx1.wait()
        left = split(jnp.concatenate([ko, -opv[:, 256:512]], axis=1))

        def known(who, carry):
            right = jnp.concatenate([lanes(tt, who), lanes(x1, who)], axis=0)
            out[0, :, chunk(who)] = mm3(left, split(right))
            return carry

        lax.fori_loop(0, 4, known, 0)
        p30.wait(ss3.at[across, 0])
        mb[0] = ss3[0, 0] + ss3[1, 0]

    eliminate(
        lambda: ss2[0, 1] + ss2[1, 1], lambda: ss2[0, 2] + ss2[1, 2], mid1, mid2, mid3, after2
    )


    def mid1():
        ph3.wait(h3.at[across])
        g3[y, c] = h3[0] + h3[1]
        gg3.start()

    def mid2():
        p3s.wait(ss3.at[across, 1 + c])
        r3s.start(lambda: ss3.at[across, 1 + c])
        r3s.wait(ss3.at[across, 2 - c])

    def mid3():
        gx2.relay()

    eliminate(
        lambda: ss3[0, 1] + ss3[1, 1], lambda: ss3[0, 2] + ss3[1, 2],
        mid1, mid2, mid3, lambda: gg3.relay((1, 3)),
    )

    def step(at, carry):
        invert_panel(mb.at[at // 2 % 2], at % 2 * PANEL)
        for k, hook in enumerate(hooks):
            pl.when(at == k)(hook)
        return carry

    lax.fori_loop(0, len(hooks), step, 0)
    k3[...] = -mm3(split(k3[...]), split(sinv[...]))
    gx2.wait()
    left = split(jnp.concatenate([k3[...], kv2[...]], axis=1))
    for d in (0, 1, 3, 2):
        who = (y + d) % 4
        if d == 2:
            gg3.relay((2,))
        gg3.wait((d,))
        right = jnp.concatenate([lanes(g3, who), -lanes(x2, who)], axis=0)
        out[0, :, chunk(who)] += mm3(left, split(right))
    for cond, make in sends:
        if cond is None:
            make().wait_send()
        else:
            pl.when(cond())(lambda make=make: make().wait_send())
    assert count[0] <= NSEM and local_count[0] <= 16


def on_device(leaf_maps, impedance, sources, top_trace, interior_op):
    anywhere = pl.BlockSpec(memory_space=pltpu.HBM)
    vm = lambda *shape: pltpu.VMEM(shape, F32)
    return pl.pallas_call(
        kernel,
        out_shape=jax.ShapeDtypeStruct((1, 256, 1024), F32),
        in_specs=[anywhere] * 5,
        out_specs=pl.BlockSpec(memory_space=pltpu.VMEM),
        scratch_shapes=[
            vm(2, 128, 128), vm(2, 128, 128), vm(2, 128, 128), vm(2, 2, 256, 128), vm(2, 256, 128),
            vm(2, 128, 128), vm(4, 2, 128, 128),
            vm(4, 2, 256, 128), vm(4, 2, 256, 128), vm(4, 2, 256, 128),
            vm(2, 1, 512), vm(2, 512, 128), vm(256, 128), vm(256, 512),
            vm(2, 3, 128, 128), vm(2, 2, 256, 128), vm(2, 2, 128, 128), vm(2, 384, 128),
            vm(2, 3, 128, 128), vm(2, 256, 128),
            vm(2, 128, 128), vm(128, 128), vm(256, 256), vm(256, 640), vm(256, 256),
            vm(256, 256), vm(256, 256),
            pltpu.SemaphoreType.DMA((NSEM,)), pltpu.SemaphoreType.DMA((16,)),
        ],
        compiler_params=pltpu.CompilerParams(
            collective_id=0, has_side_effects=True, vmem_limit_bytes=40 * 2**20
        ),
        name="merge_solve",
    )(*[pltpu.with_memory_space_constraint(a, pltpu.HBM) for a in (leaf_maps, impedance, sources, top_trace, interior_op)])


def solution(mesh):
    return jax.shard_map(
        on_device,
        mesh=mesh,
        in_specs=(
            P("sub", None, "src"),
            P("sub", None),
            P("sub", None, "src"),
            P(None, None, "src"),
            P("sub", "src", None),
        ),
        out_specs=P("sub", "src", None),
        check_vma=False,
    )
```
